32 devices in a mesh: dp: 8 (over z, y), tensor: 4 (over x, core).
Axes of the slice: x: 2, y: 2, z: 4, core: 2. Of those that a mesh axis runs over, the one named last changes fastest.
Arguments:
- layer_in: bfloat16 [8192, 1024], P(('dp', 'tensor')), may hold values from -6 to 6
- norm_gain: float32 [6, 1024], replicated, may hold values from 0.25 to 1.75
- norm_shift: float32 [6, 1024], replicated, may hold values from -2.5 to 2.5
- early_up: bfloat16 [1024, 4096], P('dp', 'tensor'), may hold values from -0.1875 to 0.1875
- early_down: bfloat16 [4096, 1024], P('tensor', 'dp'), may hold values from -0.09375 to 0.09375
- attend_in: bfloat16 [3, 1024, 1024], P(None, 'dp', 'tensor'), may hold values from -0.1875 to 0.1875
- attend_out: bfloat16 [1024, 1024], P('tensor', 'dp'), may hold values from -0.75 to 0.75
- position_table: bfloat16 [73, 64], replicated, may hold values from -4 to 4
- pointwise_in: bfloat16 [1024, 2, 1024], P('dp', None, 'tensor'), may hold values from -0.1875 to 0.1875
- depthwise: bfloat16 [31, 1024], P(None, 'tensor'), may hold values from -1 to 1
- pointwise_out: bfloat16 [1024, 1024], P('tensor', 'dp'), may hold values from -0.1875 to 0.1875
- late_up: bfloat16 [1024, 4096], P('dp', 'tensor'), may hold values from -0.1875 to 0.1875
- late_down: bfloat16 [4096, 1024], P('tensor', 'dp'), may hold values from -0.09375 to 0.09375
- output_grad: bfloat16 [8192, 1024], P(('dp', 'tensor')), may hold values from -6 to 6
- clip_lengths: int32 [16], replicated, may hold values from 128 to 512, as said below
- clip_slots: int32 [16], replicated, may hold values from 0 to 15, each once
- position_rows: int32 [73], replicated, may hold values from 0 to 72, each once
Outputs:
- layer_out: bfloat16 [8192, 1024], P(('dp', 'tensor'))
- input_grad: float32 [8192, 1024], P(('dp', 'tensor'))
- grad_norm_gain: float32 [6, 1024], replicated
- grad_norm_shift: float32 [6, 1024], replicated
- grad_early_up: float32 [1024, 4096], P('dp', 'tensor')
- grad_early_down: float32 [4096, 1024], P('tensor', 'dp')
- grad_attend_in: float32 [3, 1024, 1024], P(None, 'dp', 'tensor')
- grad_attend_out: float32 [1024, 1024], P('tensor', 'dp')
- grad_position_table: float32 [73, 64], replicated
- grad_pointwise_in: float32 [1024, 2, 1024], P('dp', None, 'tensor')
- grad_depthwise: float32 [31, 1024], replicated
- grad_pointwise_out: float32 [1024, 1024], P('tensor', 'dp')
- grad_late_up: float32 [1024, 4096], P('dp', 'tensor')
- grad_late_down: float32 [4096, 1024], P('tensor', 'dp')
The draws below stay inside these ranges and needn't reach their ends.
Inputs may be any that keep to these rules, and one draw needn't show every extreme that they name: `clip_lengths`: some clip has exactly 512 frames and some exactly 128. `clip_slots`: each slot number once. `position_rows`: each row of position_table once.
All inputs are finite; a program needn't handle non-finite values.
Results may differ from the reference program's by a relative error of at most 0.029.
Values may be sent and summed in bfloat16 or wider, within the bound.
No kernel may reach another device: no remote copies, remote signals or barrier semaphores. Data moves between devices by JAX's collectives and lax.ppermute only.
A program may use at most 192 MiB of HBM per device.

```python
import jax
import jax.numpy as jnp
from jax import lax

D = 1024
HEADS = 16
HEAD_DIM = 64
FF = 4096
KERNEL = 31
REL_LEFT = 64
REL_RIGHT = 8
NORMS = 6
CLIP_DEV = 2
L = 512
RELS = 73
NCLIP = 16
FRAMES = 8192


def draw_clip_lengths(key, part):
    key_base, key_top, key_short = jax.random.split(key, 3)
    lengths_drawn = jax.random.randint(key_base, (NCLIP,), L // 4, L + 1)
    longest = jax.random.randint(key_top, (), 0, NCLIP)
    shortest = (longest + 1 + jax.random.randint(key_short, (), 0, NCLIP - 1)) % NCLIP
    clip_ids = jnp.arange(NCLIP)
    lengths_drawn = jnp.where(clip_ids == longest, L, lengths_drawn)
    lengths_drawn = jnp.where(clip_ids == shortest, L // 4, lengths_drawn)
    return lengths_drawn.astype(jnp.int32)


def strengthened(array, stream_key, source, target, parts, factor):
    owner, partner = [(jnp.arange(array.shape[dim]) // (array.shape[dim] // parts)).reshape([-1 if axis == dim else 1 for axis in range(array.ndim)]) for dim in (source, target)]
    chosen = jax.random.permutation(stream_key, parts)[partner]
    strong = (owner == chosen) | (owner == (partner + parts // 2) % parts)
    return jnp.where(strong, factor * array, array)


def steps_of(rng, dims, shards, least, high):
    level, own = 1.0, jax.random.fold_in(rng, 6)
    for axis_at, shards_of in shards:
        draws = jnp.exp(jax.random.uniform(jax.random.fold_in(own, axis_at), (shards_of,), jnp.float32, least / len(shards), high / len(shards)))
        level = level * jnp.repeat(draws, dims[axis_at] // shards_of).reshape([-1 if axis == axis_at else 1 for axis in range(len(dims))])
    return level


def scatter_about(own_key, extent, scale, reach, cuts=(), kind=jnp.bfloat16):
    level = steps_of(own_key, extent, cuts, -0.22, 0.18) if cuts else 1.0
    values = jax.random.normal(own_key, extent, jnp.float32) * scale * level
    return jnp.minimum(jnp.maximum(values, -reach), reach).astype(kind)


def gaussian_with(own_key, shape, deviation, bound, shards, heavy, kind=jnp.bfloat16):
    values = deviation * jax.random.normal(own_key, shape, jnp.float32)
    if shards:
        values = values * steps_of(own_key, shape, shards, -0.22, 0.18)
    return jnp.clip(strengthened(values, jax.random.fold_in(own_key, 3), *heavy), -bound, bound).astype(kind)


def setup_inputs(seed: int = 0) -> dict:
    splits = jax.random.split(jax.random.key(seed), 18)
    layer_in = scatter_about(splits[0], (FRAMES, D), 1.0, 6.0, ((0, 32),))
    norm_gain = jnp.clip(1.0 + 0.15 * jax.random.normal(splits[1], (NORMS, D), jnp.float32), 0.25, 1.75)
    norm_shift = scatter_about(splits[2], (NORMS, D), 0.3, 2.5, (), jnp.float32)
    early_up = scatter_about(splits[3], (D, FF), D ** -0.5, 0.1875, ((0, 8), (1, 4)))
    early_down = scatter_about(splits[4], (FF, D), FF ** -0.5, 0.09375, ((0, 4), (1, 8)))
    attend_in = scatter_about(splits[5], (3, D, D), D ** -0.5, 0.1875, ((1, 8), (2, 4)))
    attend_out = scatter_about(splits[6], (D, D), (D // 16) ** -0.5, 0.75, ((0, 4), (1, 8)))
    position_table = scatter_about(splits[7], (RELS, HEAD_DIM), 1.0, 4.0)
    pointwise_in = scatter_about(splits[8], (D, 2, D), D ** -0.5, 0.1875, ((0, 8), (2, 4)))
    depthwise = scatter_about(splits[9], (KERNEL, D), KERNEL ** -0.5, 1.0, ((1, 4),))
    pointwise_out = scatter_about(splits[10], (D, D), D ** -0.5, 0.1875, ((0, 4), (1, 8)))
    late_up = scatter_about(splits[11], (D, FF), D ** -0.5, 0.1875, ((0, 8), (1, 4)))
    late_down = scatter_about(splits[12], (FF, D), FF ** -0.5, 0.09375, ((0, 4), (1, 8)))
    output_grad = gaussian_with(splits[13], (FRAMES, D), 1.0, 6.0, ((0, 32),), (0, 1, 32, 2.75))
    clip_lengths = draw_clip_lengths(jax.random.fold_in(splits[17], 71), 0)
    clip_slots = jax.random.permutation(splits[15], NCLIP).astype(jnp.int32)
    position_rows = jax.random.permutation(splits[16], RELS).astype(jnp.int32)
    return {"layer_in": layer_in, "norm_gain": norm_gain, "norm_shift": norm_shift, "early_up": early_up, "early_down": early_down, "attend_in": attend_in, "attend_out": attend_out, "position_table": position_table, "pointwise_in": pointwise_in, "depthwise": depthwise, "pointwise_out": pointwise_out, "late_up": late_up, "late_down": late_down, "output_grad": output_grad, "clip_lengths": clip_lengths, "clip_slots": clip_slots, "position_rows": position_rows}


@jax.custom_vjp
def low(v):
    return lax.optimization_barrier(v.astype(jnp.bfloat16)).astype(jnp.float32)

@jax.custom_vjp
def low_back(v):
    return v

def low_keep(v):
    return (low(v), None)

def low_pass(kept, grad):
    return (grad,)

def back_keep(v):
    return (v, None)

def back_low(kept, grad):
    return (low(grad),)
low.defvjp(low_keep, low_pass)
low_back.defvjp(back_keep, back_low)
norm_eps = 1e-05
masked_score = -1e+30
highest = lax.Precision.HIGHEST

def both_ways(operand):
    return low(low_back(operand))

def product(left_op, right_op):
    return jnp.dot(left_op, right_op, precision=highest, preferred_element_type=jnp.float32)

def layer_norm(operand, gain_vec, shift_vec):
    centre = operand - lax.optimization_barrier(jnp.mean(operand, axis=-1, keepdims=True))
    spread = lax.optimization_barrier(jnp.mean(centre * centre, axis=-1, keepdims=True))
    return centre * lax.rsqrt(spread + norm_eps) * gain_vec + shift_vec

def swish(operand):
    return operand * jax.nn.sigmoid(operand)

def feed_forward(stream, gain_vec, shift_vec, weight_up, weight_down):
    normed = low(layer_norm(stream, gain_vec, shift_vec))
    hidden = low_back(product(normed, weight_up))
    active = low(swish(hidden))
    return stream + low_back(0.5 * product(active, weight_down))

def attention(stream, gain_vec, shift_vec, weight_in, weight_out, pos_table, table_rows, clip_len):
    normed = low(layer_norm(stream, gain_vec, shift_vec))
    head_shape = (CLIP_DEV, L, HEADS, HEAD_DIM)
    queries = both_ways(product(normed, weight_in[0])).reshape(head_shape)
    key_rows = both_ways(product(normed, weight_in[1])).reshape(head_shape)
    values = both_ways(product(normed, weight_in[2])).reshape(head_shape)
    places = jnp.arange(L, dtype=jnp.int32)
    distance = (jnp.clip(places[None, :] - places[:, None], -REL_LEFT, REL_RIGHT) + REL_LEFT).astype(jnp.int32)
    chosen = jnp.broadcast_to(table_rows[distance].astype(jnp.int32), (CLIP_DEV, HEADS, L, L))
    by_row = jnp.einsum('cihd,rd->chir', queries, pos_table, precision=highest)
    direct = jnp.einsum('cihd,cjhd->chij', queries, key_rows, precision=highest)
    scores = low_back((direct + jnp.take_along_axis(by_row, chosen, axis=3)) * HEAD_DIM ** (-0.5))
    live_keys = places[None, :] < clip_len[:, None]
    scores = jnp.where(live_keys[:, None, None, :], scores, masked_score)
    raised = jnp.exp(scores - lax.optimization_barrier(jnp.max(scores, axis=-1, keepdims=True)))
    shares = low(raised / lax.optimization_barrier(jnp.sum(raised, axis=-1, keepdims=True)))
    attended = both_ways(jnp.einsum('chij,cjhd->cihd', shares, values, precision=highest))
    return stream + low_back(product(attended.reshape(CLIP_DEV * L, D), weight_out))

def convolution(stream, gain_vec, shift_vec, depth_gain, depth_shift, weight_in, kernel_taps, weight_out):
    normed = low(layer_norm(stream, gain_vec, shift_vec))
    halves = low_back(jnp.einsum('td,dgc->tgc', normed, weight_in, precision=highest))
    gated_rows = halves[:, 0] * jax.nn.sigmoid(halves[:, 1])
    padded = jnp.pad(gated_rows.reshape(CLIP_DEV, L, D), ((0, 0), (KERNEL - 1, 0), (0, 0)))
    convolved = kernel_taps[0] * padded[:, 0:L]
    for offset in range(1, KERNEL):
        convolved = convolved + kernel_taps[offset] * padded[:, offset:offset + L]
    active = low(swish(layer_norm(convolved.reshape(CLIP_DEV * L, D), depth_gain, depth_shift)))
    return stream + low_back(product(active, weight_out))

def layer(stream, params, clip_len, table_rows):
    gain_rows, shifts, early_up, early_down, attend_in, attend_out, pos_table, pointwise_in, depthwise, pointwise_out, late_up, late_down = params
    stream = feed_forward(stream, gain_rows[0], shifts[0], early_up, early_down)
    stream = attention(stream, gain_rows[1], shifts[1], attend_in, attend_out, pos_table, table_rows, clip_len)
    stream = convolution(stream, gain_rows[2], shifts[2], gain_rows[3], shifts[3], pointwise_in, depthwise, pointwise_out)
    stream = feed_forward(stream, gain_rows[4], shifts[4], late_up, late_down)
    return layer_norm(stream, gain_rows[5], shifts[5])

def reference(layer_in, norm_gain, norm_shift, early_up, early_down, attend_in, attend_out, position_table, pointwise_in, depthwise, pointwise_out, late_up, late_down, output_grad, clip_lengths, clip_slots, position_rows):
    groups = NCLIP // CLIP_DEV
    slot_ids = jnp.arange(NCLIP, dtype=jnp.int32)
    slot_len = lax.optimization_barrier(jnp.sum(jnp.where(clip_slots[None, :] == slot_ids[:, None], clip_lengths[None, :], 0), axis=1)).astype(jnp.int32)
    params = (norm_gain.astype(jnp.float32), norm_shift.astype(jnp.float32), early_up.astype(jnp.float32), early_down.astype(jnp.float32), attend_in.astype(jnp.float32), attend_out.astype(jnp.float32), position_table.astype(jnp.float32), pointwise_in.astype(jnp.float32), depthwise.astype(jnp.float32), pointwise_out.astype(jnp.float32), late_up.astype(jnp.float32), late_down.astype(jnp.float32))
    places = jnp.arange(L, dtype=jnp.int32)
    live_frames = (places[None, :] < slot_len[:, None]).reshape(groups, CLIP_DEV * L, 1)
    streams = layer_in.astype(jnp.float32).reshape(groups, CLIP_DEV * L, D)
    cotangents = jnp.where(live_frames, output_grad.astype(jnp.float32).reshape(groups, CLIP_DEV * L, D), 0.0)
    lengths_grouped = slot_len.reshape(groups, CLIP_DEV)

    def one_group(totals, pieces):
        stream, cotangent, clip_len = pieces
        result, pull_back = jax.vjp(lambda inputs, weights: layer(inputs, weights, clip_len, position_rows), stream, params)
        grad_stream, grad_params = pull_back(cotangent)
        return (jax.tree.map(jnp.add, totals, grad_params), (result, grad_stream))
    totals, (results, grad_streams) = lax.scan(one_group, jax.tree.map(jnp.zeros_like, params), (streams, cotangents, lengths_grouped))
    return (results.reshape(FRAMES, D).astype(jnp.bfloat16), grad_streams.reshape(FRAMES, D), totals[0], totals[1], totals[2], totals[3], totals[4], totals[5], totals[6], totals[7], totals[8], totals[9], totals[10], totals[11])
```

```python
import jax
import jax.numpy as jnp
from jax import lax
from jax.experimental import pallas as pl
from jax.experimental.pallas import tpu as pltpu
from jax.sharding import PartitionSpec as P

D = 1024
HEAD_DIM = 64
KERNEL = 31
REL_LEFT = 64
REL_RIGHT = 8
CLIP_DEV = 2
L = 512
HALF = L // 2
RELS = 73

norm_eps = 1e-05
masked_score = -1e30
highest = lax.Precision.HIGHEST
f32 = jnp.float32
bf16 = jnp.bfloat16

RING = (0, 2, 4, 6, 7, 5, 3, 1)


def mm(a, b):
    return jnp.dot(a, b, preferred_element_type=f32)


def mm_tn(a, b):
    return lax.dot_general(a, b, (((0,), (0,)), ((), ())), preferred_element_type=f32)


def mm_nt(a, b):
    return lax.dot_general(a, b, (((1,), (1,)), ((), ())), preferred_element_type=f32)


def sigmoid_parts(h):
    s = jax.nn.sigmoid(h)
    return s


def swish(h):
    return h * jax.nn.sigmoid(h)


def swish_grad(h):
    s = jax.nn.sigmoid(h)
    return s * (1.0 + h * (1.0 - s))


def to_core(v):
    return lax.ppermute(v, "tensor", [(m, m ^ 1) for m in range(lax.axis_size("tensor"))])


def to_far(v):
    return lax.ppermute(v, "tensor", [(m, m ^ 2) for m in range(lax.axis_size("tensor"))])


def to_right(v):
    n = len(RING)
    return lax.ppermute(v, "dp", [(RING[i], RING[(i + 1) % n]) for i in range(n)])


def to_left(v):
    n = len(RING)
    return lax.ppermute(v, "dp", [(RING[i], RING[(i - 1) % n]) for i in range(n)])


def on_ring():
    return lax.axis_size("dp") == len(RING)


def block_order():
    index = lax.axis_index("dp")
    count = lax.axis_size("dp")
    if not on_ring():
        return jnp.arange(count, dtype=jnp.int32)
    ring = jnp.array(RING, jnp.int32)
    place = jnp.sum(jnp.where(ring == index, jnp.arange(count, dtype=jnp.int32), 0))
    turned = (place + jnp.arange(count, dtype=jnp.int32)) % count
    return jnp.sum(jnp.where(turned[:, None] == jnp.arange(count)[None, :], ring[None, :], 0), axis=1)


def gather_rows(shard):
    if not on_ring():
        return lax.all_gather(shard, "dp", axis=0, tiled=True)
    half = shard.shape[0] // 2
    r1, l1 = to_right(shard), to_left(shard)
    r2, l2 = to_right(r1), to_left(l1)
    r3, l3 = to_right(r2), to_left(l2)
    r4, l4 = to_right(r3[:half]), to_left(l3[half:])
    return jnp.concatenate([shard, l1, l2, l3, r4, l4, r3, r2, r1], axis=0)


def scatter_rows(total):
    count = lax.axis_size("dp")
    rows = total.shape[0] // count
    if not on_ring():
        return lax.psum_scatter(total, "dp", scatter_dimension=0, tiled=True).astype(f32)
    half = rows // 2

    def block(k):
        return total[k * rows : (k + 1) * rows]

    def plus(a, b):
        return (a.astype(f32) + b.astype(f32)).astype(bf16)

    m = to_right(block(4)[:half])
    n = to_left(block(4)[half:])
    m = to_right(jnp.concatenate([plus(block(3)[:half], m), block(3)[half:]], axis=0))
    n = to_left(jnp.concatenate([block(5)[:half], plus(block(5)[half:], n)], axis=0))
    m = to_right(plus(block(2), m))
    n = to_left(plus(block(6), n))
    m = to_right(plus(block(1), m))
    n = to_left(plus(block(7), n))
    return block(0).astype(f32) + m.astype(f32) + n.astype(f32)


def sum_everywhere(values):
    def step(vals, axis, perm):
        return [v + lax.ppermute(v, axis, perm) for v in vals]

    for axis in ("tensor", "dp"):
        count = lax.axis_size(axis)
        bit = 1
        while bit < count:
            values = step(values, axis, [(m, m ^ bit) for m in range(count)])
            bit *= 2
    return values


def gather_frames(mine):
    near = to_core(mine)
    far = to_far(mine)
    return jnp.concatenate([mine, near], axis=0), jnp.concatenate([far, to_core(far)], axis=0)


def reduce_frames(own, other):
    rows = own.shape[0] // 2
    own, other = own.astype(bf16), other.astype(bf16)
    near = to_core(own[rows:])
    near_other = to_core(other[rows:])
    far = to_far((other[:rows].astype(f32) + near_other.astype(f32)).astype(bf16))
    return own[:rows].astype(f32) + near.astype(f32) + far.astype(f32)


def permute_blocks(values, order):
    count = order.shape[0]
    if not on_ring():
        return values
    width = D // count

    def body(order_ref, *refs):
        ins, outs = refs[: len(values)], refs[len(values) :]
        for src, dst in zip(ins, outs):
            for k in range(count):
                at = pl.multiple_of(order_ref[k] * width, width)
                dst[:, k * width : (k + 1) * width] = src[:, pl.ds(at, width)]

    return pl.pallas_call(
        body,
        grid_spec=pltpu.PrefetchScalarGridSpec(
            num_scalar_prefetch=1,
            grid=(),
            in_specs=[pl.BlockSpec(memory_space=pltpu.VMEM) for _ in values],
            out_specs=[pl.BlockSpec(memory_space=pltpu.VMEM) for _ in values],
        ),
        out_shape=[jax.ShapeDtypeStruct(v.shape, v.dtype) for v in values],
    )(order, *values)


def norm_forward(v, gain, shift):
    centre = v - jnp.mean(v, axis=-1, keepdims=True)
    spread = jnp.mean(centre * centre, axis=-1, keepdims=True)
    r = lax.rsqrt(spread + norm_eps)
    unit = centre * r
    return unit * gain + shift, unit, r


def norm_backward(q, unit, r, gain):
    scaled = q * gain
    bracket = (
        scaled
        - jnp.mean(scaled, axis=-1, keepdims=True)
        - unit * jnp.mean(scaled * unit, axis=-1, keepdims=True)
    )
    return r * bracket, jnp.sum(q * unit, axis=0), jnp.sum(q, axis=0)


def ffn_forward(stream, gain, shift, up, down_t):
    normed, unit, r = norm_forward(stream, gain, shift)
    frames = gather_frames(normed.astype(bf16))
    hidden = [mm(x, up) for x in frames]
    active = [swish(h).astype(bf16) for h in hidden]
    branch = reduce_frames(*[mm_nt(a, down_t) for a in active])
    return stream + 0.5 * branch, (unit, r, frames, hidden, active)


def ffn_backward(upstream, gain, up, down_t, saved):
    unit, r, frames, hidden, active = saved
    incoming = gather_frames(upstream.astype(bf16))
    dhidden = [
        (0.5 * mm(g, down_t) * swish_grad(h)).astype(bf16) for g, h in zip(incoming, hidden)
    ]
    dnormed = reduce_frames(*[mm_nt(d, up) for d in dhidden])
    grad_down = (0.5 * sum(mm_tn(g, a) for g, a in zip(incoming, active))).astype(bf16)
    grad_up = sum(mm_tn(x, d) for x, d in zip(frames, dhidden)).astype(bf16)
    dstream, dgain, dshift = norm_backward(dnormed, unit, r, gain)
    return upstream + dstream, grad_up, grad_down, dgain, dshift


def swap_halves(v, low):
    return jnp.where(low == 0, v, jnp.roll(v, HALF, axis=0))


def scores_of(q, k, table, length):
    direct = jnp.einsum("ihd,jhd->hij", q, k, preferred_element_type=f32)
    by_dist = jnp.einsum("ihd,rd->hir", q, table, preferred_element_type=f32)
    at = jnp.arange(L, dtype=jnp.int32)
    distance = jnp.clip(at[None, :] - at[:, None], -REL_LEFT, REL_RIGHT) + REL_LEFT
    band = (distance[None] == jnp.arange(RELS, dtype=jnp.int32)[:, None, None]).astype(f32)
    relative = jnp.einsum("hir,rij->hij", by_dist, band, precision=highest)
    scores = (direct + relative) * HEAD_DIM ** (-0.5)
    return jnp.where((at < length)[None, None, :], scores, masked_score), band


def attend(qkv, table, length, low):
    qkv = swap_halves(qkv, low)
    heads = qkv.shape[1] // (3 * HEAD_DIM)
    q, k, v = jnp.moveaxis(qkv.reshape(L, 3, heads, HEAD_DIM), 1, 0)
    scores, _ = scores_of(q, k, table, length)
    top = jnp.max(scores, axis=-1, keepdims=True)
    raised = jnp.exp(scores - top)
    total = jnp.sum(raised, axis=-1, keepdims=True)
    shares = (raised / total).astype(bf16)
    out = jnp.einsum("hij,jhd->ihd", shares, v, preferred_element_type=f32).astype(bf16)
    return swap_halves(out.reshape(L, heads * HEAD_DIM), low), top + jnp.log(total)


def attend_back(qkv, dout, logs, table, length, low):
    qkv = swap_halves(qkv, low)
    heads = qkv.shape[1] // (3 * HEAD_DIM)
    q, k, v = jnp.moveaxis(qkv.reshape(L, 3, heads, HEAD_DIM), 1, 0)
    dout = swap_halves(dout, low).reshape(L, heads, HEAD_DIM)
    scale = HEAD_DIM ** (-0.5)
    scores, band = scores_of(q, k, table, length)
    shares = jnp.exp(scores - logs)
    dv = jnp.einsum("hij,ihd->jhd", shares.astype(bf16), dout, preferred_element_type=f32)
    dshares = jnp.einsum("ihd,jhd->hij", dout, v, preferred_element_type=f32)
    centre = jnp.sum(shares * dshares, axis=-1, keepdims=True)
    ds = (shares * (dshares - centre)).astype(bf16)
    dq = jnp.einsum("hij,jhd->ihd", ds, k, preferred_element_type=f32) * scale
    dk = jnp.einsum("hij,ihd->jhd", ds, q, preferred_element_type=f32) * scale
    pulled = jnp.einsum("hij,rij->hir", ds.astype(f32) * scale, band, precision=highest)
    dq = dq + jnp.einsum("hir,rd->ihd", pulled, table.astype(f32), precision=highest)
    dtable = jnp.einsum("hir,ihd->rd", pulled, q.astype(f32), precision=highest)
    dqkv = jnp.stack([dq, dk, dv], axis=1).astype(bf16).reshape(L, 3 * heads * HEAD_DIM)
    return swap_halves(dqkv, low), dtable


def attention_forward(stream, gain, shift, w_in, w_out_t, table, lengths, low):
    normed, unit, r = norm_forward(stream, gain, shift)
    frames = gather_frames(normed.astype(bf16))
    qkv = [mm(x, w_in).astype(bf16) for x in frames]
    results = [attend(p, table, n, low) for p, n in zip(qkv, lengths)]
    attended = [a for a, _ in results]
    branch = reduce_frames(*[mm_nt(a, w_out_t) for a in attended])
    return stream + branch, (unit, r, frames, qkv, attended, [s for _, s in results])


def attention_backward(upstream, gain, w_in, w_out_t, table, lengths, low, saved):
    unit, r, frames, qkv, attended, logs = saved
    incoming = gather_frames(upstream.astype(bf16))
    datt = [mm(g, w_out_t).astype(bf16) for g in incoming]
    results = [
        attend_back(p, d, s, table, n, low) for p, d, s, n in zip(qkv, datt, logs, lengths)
    ]
    dqkv = [d for d, _ in results]
    dnormed = reduce_frames(*[mm_nt(d, w_in) for d in dqkv])
    grad_out = sum(mm_tn(g, a) for g, a in zip(incoming, attended)).astype(bf16)
    grad_in = sum(mm_tn(x, d) for x, d in zip(frames, dqkv)).astype(bf16)
    dtable = results[0][1] + results[1][1]
    dstream, dgain, dshift = norm_backward(dnormed, unit, r, gain)
    return upstream + dstream, grad_in, grad_out, dtable, dgain, dshift


def gated_of(halves, low):
    channels = halves.shape[1] // 2
    halves = swap_halves(halves, low)
    linear, opened = halves[:, :channels], jax.nn.sigmoid(halves[:, channels:])
    return linear, opened, jnp.pad(linear * opened, ((KERNEL - 1, 0), (0, 0)))


def convolve(padded, taps):
    out = taps[0] * padded[0:L]
    for k in range(1, KERNEL):
        out = out + taps[k] * padded[k : k + L]
    return out


def across(pairs):
    return to_far(pairs)[::-1]


def channel_stats(convolved):
    count = convolved[0].shape[1]

    def local(rows):
        mean = jnp.mean(rows, axis=-1)
        centre = rows - mean[:, None]
        return jnp.stack([mean, jnp.sum(centre * centre, axis=-1)])

    pairs = jnp.stack([local(rows) for rows in convolved])
    for send in (to_core, across):
        other = send(pairs)
        gap = pairs[:, 0] - other[:, 0]
        pairs = jnp.stack(
            [
                0.5 * (pairs[:, 0] + other[:, 0]),
                pairs[:, 1] + other[:, 1] + 0.5 * count * gap * gap,
            ],
            axis=1,
        )
        count = 2 * count
    return [(p[0][:, None], lax.rsqrt(p[1] / count + norm_eps)[:, None]) for p in pairs]


def conv_forward(stream, gain, shift, w_in, taps, w_out_t, cgain, cshift, low):
    normed, unit, r = norm_forward(stream, gain, shift)
    frames = gather_frames(normed.astype(bf16))
    opened = [gated_of(mm(x, w_in), low) for x in frames]
    convolved = [convolve(padded, taps) for _, _, padded in opened]
    parts = []
    active = []
    for gate, rows, (mean, inverse) in zip(opened, convolved, channel_stats(convolved)):
        cunit = (rows - mean) * inverse
        mid = cunit * cgain + cshift
        active.append(swap_halves(swish(mid).astype(bf16), low))
        parts.append((*gate, cunit, inverse, mid))
    branch = reduce_frames(*[mm_nt(a, w_out_t) for a in active])
    return stream + branch, (unit, r, frames, parts, active)


def conv_backward(upstream, gain, w_in, taps, w_out_t, cgain, low, saved):
    unit, r, frames, parts, active = saved
    incoming = gather_frames(upstream.astype(bf16))
    dhalves = []
    sums = []
    dmids = []
    pairs = []
    for g, (_, _, _, cunit, _, mid) in zip(incoming, parts):
        dmid = swap_halves(mm(g, w_out_t), low) * swish_grad(mid)
        scaled = dmid * cgain
        pairs.append(jnp.stack([jnp.sum(scaled, axis=-1), jnp.sum(scaled * cunit, axis=-1)]))
        dmids.append(dmid)
    pairs = jnp.stack(pairs)
    pairs = pairs + to_core(pairs)
    pairs = (pairs + across(pairs)) / D
    for dmid, pair, (linear, opened, padded, cunit, inverse, mid) in zip(dmids, pairs, parts):
        scaled = dmid * cgain
        dconv = inverse * (scaled - pair[0][:, None] - cunit * pair[1][:, None])
        late = jnp.pad(dconv, ((0, KERNEL - 1), (0, 0)))
        dgated = taps[0] * late[KERNEL - 1 : KERNEL - 1 + L]
        for k in range(1, KERNEL):
            dgated = dgated + taps[k] * late[KERNEL - 1 - k : KERNEL - 1 - k + L]
        dtaps = jnp.stack([jnp.sum(padded[k : k + L] * dconv, axis=0) for k in range(KERNEL)])
        dh = jnp.concatenate(
            [dgated * opened, dgated * linear * opened * (1.0 - opened)], axis=1
        ).astype(bf16)
        dhalves.append(swap_halves(dh, low))
        sums.append((dtaps, jnp.sum(dmid * cunit, axis=0), jnp.sum(dmid, axis=0)))
    dnormed = reduce_frames(*[mm_nt(d, w_in) for d in dhalves])
    grad_out = sum(mm_tn(g, a) for g, a in zip(incoming, active)).astype(bf16)
    grad_in = sum(mm_tn(x, d) for x, d in zip(frames, dhalves)).astype(bf16)
    dtaps, dcgain, dcshift = [a + b for a, b in zip(*sums)]
    dstream, dgain, dshift = norm_backward(dnormed, unit, r, gain)
    return upstream + dstream, grad_in, grad_out, dtaps, dgain, dshift, dcgain, dcshift


def spread_channels(part, member):
    zero = jnp.zeros(part.shape[:-1] + (D,), f32)
    return lax.dynamic_update_slice_in_dim(zero, part, member * part.shape[-1], part.ndim - 1)


def per_device(
    layer_in,
    norm_gain,
    norm_shift,
    early_up,
    early_down,
    attend_in,
    attend_out,
    position_table,
    pointwise_in,
    depthwise,
    pointwise_out,
    late_up,
    late_down,
    output_grad,
    clip_lengths,
    clip_slots,
    position_rows,
):
    group = lax.axis_index("dp")
    member = lax.axis_index("tensor")
    low = member % 2
    high = member // 2
    rows_here = layer_in.shape[0]
    block = early_up.shape[0]
    channels = depthwise.shape[1]

    order = block_order()
    count = order.shape[0]
    inverse_order = jnp.sum(
        jnp.where(
            order[None, :] == jnp.arange(count, dtype=jnp.int32)[:, None],
            jnp.arange(count, dtype=jnp.int32)[None, :],
            0,
        ),
        axis=1,
    )
    stream, cotangent, gains, shifts = permute_blocks(
        [layer_in, output_grad, norm_gain, norm_shift], order
    )

    slots = group * CLIP_DEV + jnp.stack([high, 1 - high])
    lengths = jnp.sum(
        jnp.where(clip_slots[None, :] == slots[:, None], clip_lengths[None, :], 0), axis=1
    )
    lengths = [lengths[0], lengths[1]]
    live = low * rows_here + jnp.arange(rows_here, dtype=jnp.int32) < lengths[0]

    selector = (position_rows[:, None] == jnp.arange(RELS, dtype=jnp.int32)[None, :]).astype(f32)
    table = jnp.dot(selector, position_table.astype(f32), precision=highest).astype(bf16)
    cgain = lax.dynamic_slice_in_dim(norm_gain[3], member * channels, channels)
    cshift = lax.dynamic_slice_in_dim(norm_shift[3], member * channels, channels)
    taps = depthwise.astype(f32)

    pack_attend = jnp.concatenate(
        [jnp.moveaxis(attend_in, 0, 1).reshape(block, -1), attend_out.T], axis=1
    )
    pack_conv = jnp.concatenate([pointwise_in.reshape(block, -1), pointwise_out.T], axis=1)
    wide = attend_in.shape[0] * attend_in.shape[2]
    cwide = 2 * channels

    w_early_up = gather_rows(early_up)
    w_early_down = gather_rows(early_down.T)
    w_attend = gather_rows(pack_attend)
    w_conv = gather_rows(pack_conv)
    w_late_up = gather_rows(late_up)
    w_late_down = gather_rows(late_down.T)
    w_att_in, w_att_out = w_attend[:, :wide], w_attend[:, wide:]
    w_pi, w_po = w_conv[:, :cwide], w_conv[:, cwide:]

    stream0 = stream.astype(f32)
    stream1, saved_early = ffn_forward(stream0, gains[0], shifts[0], w_early_up, w_early_down)
    stream2, saved_attend = attention_forward(
        stream1, gains[1], shifts[1], w_att_in, w_att_out, table, lengths, low
    )
    stream3, saved_conv = conv_forward(
        stream2, gains[2], shifts[2], w_pi, taps, w_po, cgain, cshift, low
    )
    stream4, saved_late = ffn_forward(stream3, gains[4], shifts[4], w_late_up, w_late_down)
    result, unit5, r5 = norm_forward(stream4, gains[5], shifts[5])

    up = jnp.where(live[:, None], cotangent.astype(f32), 0.0)
    up, gain5, shift5 = norm_backward(up, unit5, r5, gains[5])
    up, g_late_up, g_late_down, gain4, shift4 = ffn_backward(
        up, gains[4], w_late_up, w_late_down, saved_late
    )
    g_late_up = scatter_rows(g_late_up)
    g_late_down = scatter_rows(g_late_down)
    up, g_pi, g_po, g_taps, gain2, shift2, gain3, shift3 = conv_backward(
        up, gains[2], w_pi, taps, w_po, cgain, low, saved_conv
    )
    g_conv = scatter_rows(jnp.concatenate([g_pi, g_po], axis=1))
    up, g_in, g_out, g_table, gain1, shift1 = attention_backward(
        up, gains[1], w_att_in, w_att_out, table, lengths, low, saved_attend
    )
    g_attend = scatter_rows(jnp.concatenate([g_in, g_out], axis=1))
    up, g_early_up, g_early_down, gain0, shift0 = ffn_backward(
        up, gains[0], w_early_up, w_early_down, saved_early
    )
    g_early_down = scatter_rows(g_early_down)
    g_early_up = scatter_rows(g_early_up)

    zero_row = jnp.zeros((D,), f32)
    norms = jnp.stack(
        [gain0, gain1, gain2, zero_row, gain4, gain5, shift0, shift1, shift2, zero_row, shift4, shift5]
    )
    result, up, norms = permute_blocks([result.astype(bf16), up, norms], inverse_order)
    side = spread_channels(jnp.concatenate([g_taps, gain3[None], shift3[None]], axis=0), member)
    table_part = jnp.dot(selector.T, g_table, precision=highest)
    norms, side, table_all = sum_everywhere([norms, side, table_part])
    gains_all = jnp.concatenate([norms[0:3], side[KERNEL : KERNEL + 1], norms[4:6]], axis=0)
    shifts_all = jnp.concatenate([norms[6:9], side[KERNEL + 1 :], norms[10:12]], axis=0)

    return (
        result,
        up,
        gains_all,
        shifts_all,
        g_early_up,
        g_early_down.T,
        jnp.moveaxis(g_attend[:, :wide].reshape(block, 3, -1), 1, 0),
        g_attend[:, wide:].T,
        table_all,
        g_conv[:, :cwide].reshape(block, 2, channels),
        side[:KERNEL],
        g_conv[:, cwide:].T,
        g_late_up,
        g_late_down.T,
    )


def solution(mesh):
    return jax.shard_map(
        per_device,
        mesh=mesh,
        in_specs=(
            P(("dp", "tensor"), None),
            P(),
            P(),
            P("dp", "tensor"),
            P("tensor", "dp"),
            P(None, "dp", "tensor"),
            P("tensor", "dp"),
            P(),
            P("dp", None, "tensor"),
            P(None, "tensor"),
            P("tensor", "dp"),
            P("dp", "tensor"),
            P("tensor", "dp"),
            P(("dp", "tensor"), None),
            P(),
            P(),
            P(),
        ),
        out_specs=(
            P(("dp", "tensor"), None),
            P(("dp", "tensor"), None),
            P(),
            P(),
            P("dp", "tensor"),
            P("tensor", "dp"),
            P(None, "dp", "tensor"),
            P("tensor", "dp"),
            P(),
            P("dp", None, "tensor"),
            P(),
            P("tensor", "dp"),
            P("dp", "tensor"),
            P("tensor", "dp"),
        ),
        check_vma=False,
    )
```

```python
import jax
import jax.numpy as jnp
from jax import lax
from jax.experimental import pallas as pl
from jax.experimental.pallas import tpu as pltpu
from jax.sharding import PartitionSpec as P

D = 1024
HEAD_DIM = 64
KERNEL = 31
REL_LEFT = 64
REL_RIGHT = 8
CLIP_DEV = 2
L = 512
HALF = L // 2
RELS = 73

norm_eps = 1e-05
masked_score = -1e30
highest = lax.Precision.HIGHEST
f32 = jnp.float32
bf16 = jnp.bfloat16

RING = (0, 2, 4, 6, 7, 5, 3, 1)


def mm(a, b):
    return jnp.dot(a, b, preferred_element_type=f32)


def mm_tn(a, b):
    return lax.dot_general(a, b, (((0,), (0,)), ((), ())), preferred_element_type=f32)


def mm_nt(a, b):
    return lax.dot_general(a, b, (((1,), (1,)), ((), ())), preferred_element_type=f32)


def swish(h):
    return h * jax.nn.sigmoid(h)


def swish_grad(h):
    s = jax.nn.sigmoid(h)
    return s * (1.0 + h * (1.0 - s))


def to_core(v):
    return lax.ppermute(v, "tensor", [(m, m ^ 1) for m in range(lax.axis_size("tensor"))])


def to_far(v):
    return lax.ppermute(v, "tensor", [(m, m ^ 2) for m in range(lax.axis_size("tensor"))])


def to_right(v):
    n = len(RING)
    return lax.ppermute(v, "dp", [(RING[i], RING[(i + 1) % n]) for i in range(n)])


def to_left(v):
    n = len(RING)
    return lax.ppermute(v, "dp", [(RING[i], RING[(i - 1) % n]) for i in range(n)])


def on_ring():
    return lax.axis_size("dp") == len(RING)


def block_order():
    index = lax.axis_index("dp")
    count = lax.axis_size("dp")
    if not on_ring():
        return jnp.arange(count, dtype=jnp.int32)
    ring = jnp.array(RING, jnp.int32)
    place = jnp.sum(jnp.where(ring == index, jnp.arange(count, dtype=jnp.int32), 0))
    turned = (place + jnp.arange(count, dtype=jnp.int32)) % count
    return jnp.sum(jnp.where(turned[:, None] == jnp.arange(count)[None, :], ring[None, :], 0), axis=1)


def after(values, signal):
    return lax.optimization_barrier((values, signal))[0]


def gather_rows(shard):
    if not on_ring():
        return [lax.all_gather(shard, "dp", axis=0, tiled=True)], shard
    half = shard.shape[0] // 2
    r1, l1 = to_right(shard), to_left(shard)
    r2, l2 = to_right(r1), to_left(l1)
    r3, l3 = to_right(r2), to_left(l2)
    r4, l4 = to_right(r3[:half]), to_left(l3[half:])
    return [shard, l1, l2, l3, r4, l4, r3, r2, r1], (r3[:8], l3[:8])


def columns(pieces, start, stop):
    return jnp.concatenate([p[:, start:stop] for p in pieces], axis=0)


def scatter_rows(totals, signal):
    count = lax.axis_size("dp")
    rows = totals[0].shape[0] // count
    if not on_ring():
        total = jnp.concatenate(totals, axis=1)
        return lax.psum_scatter(total, "dp", scatter_dimension=0, tiled=True).astype(f32), signal
    half = rows // 2

    def part(start, stop):
        return jnp.concatenate([t[start:stop] for t in totals], axis=1)

    def block(k):
        return part(k * rows, (k + 1) * rows)

    def plus(a, b):
        return (a.astype(f32) + b.astype(f32)).astype(bf16)

    right, left = part(4 * rows, 4 * rows + half), part(4 * rows + half, 5 * rows)
    if signal is not None:
        right, left = after((right, left), signal)
    m = to_right(right)
    n = to_left(left)
    m = to_right(
        jnp.concatenate(
            [plus(part(3 * rows, 3 * rows + half), m), part(3 * rows + half, 4 * rows)], axis=0
        )
    )
    n = to_left(
        jnp.concatenate(
            [part(5 * rows, 5 * rows + half), plus(part(5 * rows + half, 6 * rows), n)], axis=0
        )
    )
    m = to_right(plus(block(2), m))
    n = to_left(plus(block(6), n))
    free = (m[:8], n[:8])
    m = to_right(plus(block(1), m))
    n = to_left(plus(block(7), n))
    return block(0).astype(f32) + m.astype(f32) + n.astype(f32), free


def sum_everywhere(value):
    for axis in ("tensor", "dp"):
        count = lax.axis_size(axis)
        bit = 1
        while bit < count:
            value = value + lax.ppermute(value, axis, [(m, m ^ bit) for m in range(count)])
            bit *= 2
    return value


def gather_clip(mine):
    return jnp.concatenate([mine, to_core(mine)], axis=0)


def reduce_clip(partial):
    rows = partial.shape[0] // 2
    partial = partial.astype(bf16)
    return partial[:rows].astype(f32) + to_core(partial[rows:]).astype(f32)


def gather_frames(mine):
    near = to_core(mine)
    far = to_far(mine)
    return jnp.concatenate([mine, near], axis=0), jnp.concatenate([far, to_core(far)], axis=0)


def reduce_frames(own, other):
    rows = own.shape[0] // 2
    own, other = own.astype(bf16), other.astype(bf16)
    near = to_core(own[rows:])
    near_other = to_core(other[rows:])
    far = to_far((other[:rows].astype(f32) + near_other.astype(f32)).astype(bf16))
    return own[:rows].astype(f32) + near.astype(f32) + far.astype(f32)


def permute_blocks(values, order):
    count = order.shape[0]
    if not on_ring():
        return values
    width = D // count

    def body(order_ref, *refs):
        ins, outs = refs[: len(values)], refs[len(values) :]
        for src, dst in zip(ins, outs):
            for k in range(count):
                at = pl.multiple_of(order_ref[k] * width, width)
                dst[:, k * width : (k + 1) * width] = src[:, pl.ds(at, width)]

    return pl.pallas_call(
        body,
        grid_spec=pltpu.PrefetchScalarGridSpec(
            num_scalar_prefetch=1,
            grid=(),
            in_specs=[pl.BlockSpec(memory_space=pltpu.VMEM) for _ in values],
            out_specs=[pl.BlockSpec(memory_space=pltpu.VMEM) for _ in values],
        ),
        out_shape=[jax.ShapeDtypeStruct(v.shape, v.dtype) for v in values],
    )(order, *values)


def norm_forward(v, gain, shift):
    centre = v - jnp.mean(v, axis=-1, keepdims=True)
    spread = jnp.mean(centre * centre, axis=-1, keepdims=True)
    r = lax.rsqrt(spread + norm_eps)
    unit = centre * r
    return unit * gain + shift, unit, r


def norm_backward(q, unit, r, gain):
    scaled = q * gain
    bracket = (
        scaled
        - jnp.mean(scaled, axis=-1, keepdims=True)
        - unit * jnp.mean(scaled * unit, axis=-1, keepdims=True)
    )
    return r * bracket, jnp.sum(q * unit, axis=0), jnp.sum(q, axis=0)


def ffn_forward(stream, gain, shift, up, down_t):
    normed, unit, r = norm_forward(stream, gain, shift)
    frames = gather_frames(normed.astype(bf16))
    hidden = [mm(x, up) for x in frames]
    active = [swish(h).astype(bf16) for h in hidden]
    branch = reduce_frames(*[mm_nt(a, down_t) for a in active])
    return stream + 0.5 * branch, (unit, r, frames, hidden, active)


def ffn_backward(upstream, gain, up, down_t, saved):
    unit, r, frames, hidden, active = saved
    incoming = gather_frames(upstream.astype(bf16))
    dhidden = [
        (0.5 * mm(g, down_t) * swish_grad(h)).astype(bf16) for g, h in zip(incoming, hidden)
    ]
    dnormed = reduce_frames(*[mm_nt(d, up) for d in dhidden])
    grad_down = (0.5 * sum(mm_tn(g, a) for g, a in zip(incoming, active))).astype(bf16)
    grad_up = sum(mm_tn(x, d) for x, d in zip(frames, dhidden)).astype(bf16)
    dstream, dgain, dshift = norm_backward(dnormed, unit, r, gain)
    return upstream + dstream, grad_up, grad_down, dgain, dshift


LANES = 128
SCALE = HEAD_DIM ** (-0.5)


def head_lanes(value, upper):
    lane = lax.broadcasted_iota(jnp.int32, value.shape, 1)
    return jnp.where((lane >= HEAD_DIM) == upper, value, jnp.zeros_like(value))


def either(first, second):
    lane = lax.broadcasted_iota(jnp.int32, first.shape, 1)
    return jnp.where(lane < HEAD_DIM, first, second)


def tile_probs(meta_ref, q, k, table):
    low, length = meta_ref[0], meta_ref[1]
    place_i = (lax.broadcasted_iota(jnp.int32, (L, L), 0) + low * HALF) & (L - 1)
    place_j = (lax.broadcasted_iota(jnp.int32, (L, L), 1) + low * HALF) & (L - 1)
    offset = place_j - place_i
    by_row = mm_nt(q, table)
    turned = pltpu.roll(by_row, REL_LEFT, 1, stride=1, stride_axis=0)
    turned = jnp.concatenate([turned] * (L // LANES), axis=1)
    relative = jnp.where(
        offset < -REL_LEFT,
        by_row[:, :1],
        jnp.where(offset >= LANES - REL_LEFT, by_row[:, LANES - 1 :], turned),
    )
    scores = (mm_nt(q, k) + relative) * SCALE
    scores = jnp.where(place_j < length, scores, masked_score)
    raised = jnp.exp(scores - jnp.max(scores, axis=-1, keepdims=True))
    return raised / jnp.sum(raised, axis=-1, keepdims=True), offset


def attend_body(meta_ref, q_ref, k_ref, v_ref, table_ref, out_ref):
    q, k, v, table = q_ref[...], k_ref[...], v_ref[...], table_ref[...]
    outs = []
    for upper in (False, True):
        shares, _ = tile_probs(meta_ref, head_lanes(q, upper), k, table)
        outs.append(mm(shares.astype(bf16), v))
    out_ref[...] = either(*outs).astype(bf16)


def pair_specs(pairs):
    def at(which):
        return pl.BlockSpec((L, LANES), lambda n, meta: (0, which * pairs + n))

    return [at(0), at(1), at(2)]


def attend(qkv, table, meta):
    width = qkv.shape[1] // 3
    pairs = width // LANES
    return pl.pallas_call(
        attend_body,
        grid_spec=pltpu.PrefetchScalarGridSpec(
            num_scalar_prefetch=1,
            grid=(pairs,),
            in_specs=pair_specs(pairs) + [pl.BlockSpec((LANES, LANES), lambda n, meta: (0, 0))],
            out_specs=pl.BlockSpec((L, LANES), lambda n, meta: (0, n)),
        ),
        out_shape=jax.ShapeDtypeStruct((L, width), bf16),
    )(meta, qkv, qkv, qkv, table)


def attend_back_body(
    meta_ref, q_ref, k_ref, v_ref, do_ref, table_ref, dq_ref, dk_ref, dv_ref, dtable_ref
):
    q, k, v, do, table = q_ref[...], k_ref[...], v_ref[...], do_ref[...], table_ref[...]
    lane = lax.broadcasted_iota(jnp.int32, (L, LANES), 1)
    row = lax.broadcasted_iota(jnp.int32, (L, LANES), 0)
    dqs, dks, dvs = [], [], []
    dtable = jnp.zeros((LANES, LANES), f32)
    for upper in (False, True):
        q_one = head_lanes(q, upper)
        shares, offset = tile_probs(meta_ref, q_one, k, table)
        dvs.append(mm_tn(shares.astype(bf16), do))
        dshares = mm_nt(head_lanes(do, upper), v)
        centre = jnp.sum(shares * dshares, axis=-1, keepdims=True)
        ds = (shares * (dshares - centre)).astype(bf16)
        wide = ds.astype(f32)
        before = offset < -REL_LEFT
        beyond = offset >= LANES - REL_LEFT
        left = jnp.sum(jnp.where(before, wide, 0.0), axis=-1, keepdims=True)
        right = jnp.sum(jnp.where(beyond, wide, 0.0), axis=-1, keepdims=True)
        band = jnp.where(before | beyond, 0.0, wide)
        pulled = sum(band[:, n * LANES : (n + 1) * LANES] for n in range(L // LANES))
        pulled = pltpu.roll(pulled, LANES - REL_LEFT, 1)
        bit = 1
        while bit < LANES:
            pulled = jnp.where((row & bit) != 0, pltpu.roll(pulled, LANES - bit, 1), pulled)
            bit *= 2
        pulled = pulled + jnp.where(lane == 0, left, 0.0) + jnp.where(lane == LANES - 1, right, 0.0)
        pulled = pulled.astype(bf16)
        dqs.append(mm(ds, k) + mm(pulled, table))
        dks.append(mm_tn(ds, q))
        dtable = dtable + mm_tn(pulled, q_one)
    dq_ref[...] = (either(*dqs) * SCALE).astype(bf16)
    dk_ref[...] = (either(*dks) * SCALE).astype(bf16)
    dv_ref[...] = either(*dvs).astype(bf16)

    @pl.when(pl.program_id(0) == 0)
    def _():
        dtable_ref[...] = jnp.zeros_like(dtable_ref)

    dtable_ref[...] += dtable * SCALE


def attend_back(qkv, dout, table, meta):
    width = qkv.shape[1] // 3
    pairs = width // LANES
    pair = pl.BlockSpec((L, LANES), lambda n, meta: (0, n))
    square = pl.BlockSpec((LANES, LANES), lambda n, meta: (0, 0))
    part = jax.ShapeDtypeStruct((L, width), bf16)
    return pl.pallas_call(
        attend_back_body,
        grid_spec=pltpu.PrefetchScalarGridSpec(
            num_scalar_prefetch=1,
            grid=(pairs,),
            in_specs=pair_specs(pairs) + [pair, square],
            out_specs=[pair, pair, pair, square],
        ),
        out_shape=[part, part, part, jax.ShapeDtypeStruct((LANES, LANES), f32)],
    )(meta, qkv, qkv, qkv, dout, table)


def attention_forward(stream, gain, shift, w_in, w_out_t, table, meta):
    normed, unit, r = norm_forward(stream, gain, shift)
    frames = gather_clip(normed.astype(bf16))
    qkv = mm(frames, w_in).astype(bf16)
    attended = attend(qkv, table, meta)
    branch = reduce_clip(mm_nt(attended, w_out_t))
    return stream + branch, (unit, r, frames, qkv, attended)


def attention_backward(upstream, gain, w_in, w_out_t, table, meta, saved):
    unit, r, frames, qkv, attended = saved
    incoming = gather_clip(upstream.astype(bf16))
    datt = mm(incoming, w_out_t).astype(bf16)
    dq, dk, dv, dtable = attend_back(qkv, datt, table, meta)
    width = dq.shape[1]
    dnormed = reduce_clip(
        sum(mm_nt(d, w_in[:, n * width : (n + 1) * width]) for n, d in enumerate((dq, dk, dv)))
    )
    grads = [mm_tn(frames, d).astype(bf16) for d in (dq, dk, dv)]
    grads.append(mm_tn(incoming, attended).astype(bf16))
    dstream, dgain, dshift = norm_backward(dnormed, unit, r, gain)
    return upstream + dstream, grads, dtable, dgain, dshift


PAD = 32
CHUNK = 64


def place_rows(dst, value, start, low):
    own = pl.multiple_of(start + low * HALF, 8)
    other = pl.multiple_of(start + (1 - low) * HALF, 8)
    dst[pl.ds(own, HALF), :] = value[:HALF]
    dst[pl.ds(other, HALF), :] = value[HALF:]


def taken_rows(src, start, low):
    own = pl.multiple_of(start + low * HALF, 8)
    other = pl.multiple_of(start + (1 - low) * HALF, 8)
    return src[pl.ds(own, HALF), :], src[pl.ds(other, HALF), :]


def shifted(window, shift):
    size = window.shape[0]
    turned = {}

    def at(first):
        part = first % 8
        if part not in turned:
            turned[part] = window if part == 0 else pltpu.roll(window, size - part, 0)
        base = first - part
        return turned[part][base : base + CHUNK]

    return at


def conv_body(meta_ref, linear_ref, gate_ref, taps_ref, out_ref, padded, placed):
    low = meta_ref[0]
    padded[:PAD, :] = jnp.zeros((PAD, LANES), f32)
    place_rows(padded, linear_ref[...] * jax.nn.sigmoid(gate_ref[...]), PAD, low)
    taps = taps_ref[...]

    def chunk(c, carry):
        base = pl.multiple_of(c * CHUNK, CHUNK)
        at = shifted(padded[pl.ds(base, CHUNK + PAD), :], 0)
        total = taps[0:1] * at(2)
        for k in range(1, KERNEL):
            total = total + taps[k : k + 1] * at(2 + k)
        placed[pl.ds(base, CHUNK), :] = total
        return carry

    lax.fori_loop(0, L // CHUNK, chunk, 0)
    out_ref[:HALF, :], out_ref[HALF:, :] = taken_rows(placed, 0, low)


def conv_back_body(
    meta_ref, dconv_ref, linear_ref, gate_ref, taps_ref, dlin_ref, dgate_ref, dtaps_ref, padded, late, placed
):
    low = meta_ref[0]
    linear, opened = linear_ref[...], jax.nn.sigmoid(gate_ref[...])
    padded[:PAD, :] = jnp.zeros((PAD, LANES), f32)
    place_rows(padded, linear * opened, PAD, low)
    late[L:, :] = jnp.zeros((PAD, LANES), f32)
    place_rows(late, dconv_ref[...], 0, low)
    taps = taps_ref[...]
    dtaps_ref[...] = jnp.zeros_like(dtaps_ref)

    def chunk(c, carry):
        base = pl.multiple_of(c * CHUNK, CHUNK)
        window = late[pl.ds(base, CHUNK + PAD), :]
        ahead = shifted(window, 0)
        back = shifted(padded[pl.ds(base, CHUNK + PAD), :], 0)
        here = window[:CHUNK]
        total = taps[KERNEL - 1 : KERNEL] * here
        for k in range(KERNEL - 1):
            total = total + taps[k : k + 1] * ahead(KERNEL - 1 - k)
        placed[pl.ds(base, CHUNK), :] = total
        for k in range(KERNEL):
            part = (back(2 + k) * here).reshape(CHUNK // 8, 8, LANES)
            dtaps_ref[8 * k : 8 * k + 8, :] += jnp.sum(part, axis=0)
        return carry

    lax.fori_loop(0, L // CHUNK, chunk, 0)
    dgated = jnp.concatenate(taken_rows(placed, 0, low), axis=0)
    dlin_ref[...] = (dgated * opened).astype(bf16)
    dgate_ref[...] = (dgated * linear * opened * (1.0 - opened)).astype(bf16)


def conv_specs(blocks):
    linear = pl.BlockSpec((L, LANES), lambda n, meta: (0, n))
    gate = pl.BlockSpec((L, LANES), lambda n, meta: (0, blocks + n))
    taps = pl.BlockSpec((PAD, LANES), lambda n, meta: (0, n))
    return linear, gate, taps


def conv_gated(halves, taps, meta):
    width = halves.shape[1] // 2
    linear, gate, tap = conv_specs(width // LANES)
    return pl.pallas_call(
        conv_body,
        grid_spec=pltpu.PrefetchScalarGridSpec(
            num_scalar_prefetch=1,
            grid=(width // LANES,),
            in_specs=[linear, gate, tap],
            out_specs=linear,
            scratch_shapes=[pltpu.VMEM((L + PAD, LANES), f32), pltpu.VMEM((L, LANES), f32)],
        ),
        out_shape=jax.ShapeDtypeStruct((L, width), f32),
    )(meta, halves, halves, taps)


def conv_gated_back(dconv, halves, taps, meta):
    width = dconv.shape[1]
    linear, gate, tap = conv_specs(width // LANES)
    long = pltpu.VMEM((L + PAD, LANES), f32)
    return pl.pallas_call(
        conv_back_body,
        grid_spec=pltpu.PrefetchScalarGridSpec(
            num_scalar_prefetch=1,
            grid=(width // LANES,),
            in_specs=[linear, linear, gate, tap],
            out_specs=[linear, linear, pl.BlockSpec((8 * PAD, LANES), lambda n, meta: (0, n))],
            scratch_shapes=[long, long, pltpu.VMEM((L, LANES), f32)],
        ),
        out_shape=[
            jax.ShapeDtypeStruct((L, width), bf16),
            jax.ShapeDtypeStruct((L, width), bf16),
            jax.ShapeDtypeStruct((8 * PAD, width), f32),
        ],
    )(meta, dconv, halves, halves, taps)


def near_rows(pair):
    return jnp.roll(to_core(pair), HALF, axis=-1)


def channel_stats(convolved):
    count = convolved.shape[1]
    mean = jnp.mean(convolved, axis=-1)
    centre = convolved - mean[:, None]
    pair = jnp.stack([mean, jnp.sum(centre * centre, axis=-1)])
    other = near_rows(pair)
    gap = pair[0] - other[0]
    mean = 0.5 * (pair[0] + other[0])
    spread = (pair[1] + other[1] + 0.5 * count * gap * gap) / (2 * count)
    return mean[:, None], lax.rsqrt(spread + norm_eps)[:, None]


def conv_forward(stream, gain, shift, w_in, taps, w_out_t, cgain, cshift, meta):
    normed, unit, r = norm_forward(stream, gain, shift)
    frames = gather_clip(normed.astype(bf16))
    halves = mm(frames, w_in)
    convolved = conv_gated(halves, taps, meta)
    mean, inverse = channel_stats(convolved)
    cunit = (convolved - mean) * inverse
    active = swish(cunit * cgain + cshift).astype(bf16)
    branch = reduce_clip(mm_nt(active, w_out_t))
    return stream + branch, (unit, r, frames, halves, cunit, inverse, active)


def conv_backward(upstream, gain, w_in, taps, w_out_t, cgain, cshift, meta, saved):
    unit, r, frames, halves, cunit, inverse, active = saved
    incoming = gather_clip(upstream.astype(bf16))
    dmid = mm(incoming, w_out_t) * swish_grad(cunit * cgain + cshift)
    scaled = dmid * cgain
    pair = jnp.stack([jnp.sum(scaled, axis=-1), jnp.sum(scaled * cunit, axis=-1)])
    pair = (pair + near_rows(pair)) / D
    dconv = inverse * (scaled - pair[0][:, None] - cunit * pair[1][:, None])
    dlin, dgate, dtaps = conv_gated_back(dconv, halves, taps, meta)
    width = dlin.shape[1]
    dnormed = reduce_clip(mm_nt(dlin, w_in[:, :width]) + mm_nt(dgate, w_in[:, width:]))
    grads = [mm_tn(frames, d).astype(bf16) for d in (dlin, dgate)]
    grads.append(mm_tn(incoming, active).astype(bf16))
    dtaps = jnp.sum(dtaps.reshape(PAD, 8, width), axis=1)[:KERNEL]
    sums = (dtaps, jnp.sum(dmid * cunit, axis=0), jnp.sum(dmid, axis=0))
    dstream, dgain, dshift = norm_backward(dnormed, unit, r, gain)
    return upstream + dstream, grads, sums, dgain, dshift


def spread_channels(part, member):
    zero = jnp.zeros(part.shape[:-1] + (D,), f32)
    return lax.dynamic_update_slice_in_dim(zero, part, member * part.shape[-1], part.ndim - 1)


def per_device(
    layer_in,
    norm_gain,
    norm_shift,
    early_up,
    early_down,
    attend_in,
    attend_out,
    position_table,
    pointwise_in,
    depthwise,
    pointwise_out,
    late_up,
    late_down,
    output_grad,
    clip_lengths,
    clip_slots,
    position_rows,
):
    group = lax.axis_index("dp")
    member = lax.axis_index("tensor")
    low = member % 2
    high = member // 2
    rows_here = layer_in.shape[0]
    block = early_up.shape[0]
    channels = depthwise.shape[1]

    order = block_order()
    count = order.shape[0]
    inverse_order = jnp.sum(
        jnp.where(
            order[None, :] == jnp.arange(count, dtype=jnp.int32)[:, None],
            jnp.arange(count, dtype=jnp.int32)[None, :],
            0,
        ),
        axis=1,
    )
    stream, cotangent, gains, shifts = permute_blocks(
        [layer_in, output_grad, norm_gain, norm_shift], order
    )

    slot = group * CLIP_DEV + high
    length = jnp.sum(jnp.where(clip_slots == slot, clip_lengths, 0))
    live = low * rows_here + jnp.arange(rows_here, dtype=jnp.int32) < length
    meta = jnp.stack([low, length]).astype(jnp.int32)

    selector = (position_rows[:, None] == jnp.arange(RELS, dtype=jnp.int32)[None, :]).astype(f32)
    table = jnp.dot(selector, position_table.astype(f32), precision=highest).astype(bf16)
    table = jnp.concatenate([table, jnp.broadcast_to(table[-1:], (LANES - RELS, HEAD_DIM))], axis=0)
    table = jnp.concatenate([table, table], axis=1)

    far_member = member ^ 2

    def both_members(row):
        return jnp.concatenate(
            [
                lax.dynamic_slice_in_dim(row, at * channels, channels)
                for at in (member, far_member)
            ]
        )

    cgain, cshift = both_members(norm_gain[3]), both_members(norm_shift[3])

    pack_attend = jnp.concatenate(
        [jnp.moveaxis(attend_in, 0, 1).reshape(block, -1), attend_out.T], axis=1
    )
    pack_conv = jnp.concatenate([pointwise_in.reshape(block, -1), pointwise_out.T], axis=1)
    far_attend = to_far(pack_attend)
    far_conv = to_far(pack_conv)
    taps = jnp.concatenate([depthwise, to_far(depthwise)], axis=1).astype(f32)
    taps = jnp.pad(taps, ((0, PAD - KERNEL), (0, 0)))

    def paired(own, far):
        parts = []
        for at in range(0, own.shape[1], channels):
            parts += [own[:, at : at + channels], far[:, at : at + channels]]
        return jnp.concatenate(parts, axis=1)

    both = 2 * channels
    p_early_up, signal = gather_rows(early_up)
    p_early_down, signal = gather_rows(after(early_down.T, signal))
    p_attend, signal = gather_rows(after(paired(pack_attend, far_attend), signal))
    p_conv, signal = gather_rows(after(paired(pack_conv, far_conv), signal))
    p_late, signal = gather_rows(after(jnp.concatenate([late_up, late_down.T], axis=1), signal))
    hidden_cols = early_up.shape[1]
    w_early_up = columns(p_early_up, 0, hidden_cols)
    w_early_down = columns(p_early_down, 0, hidden_cols)
    w_att_in, w_att_out = columns(p_attend, 0, 3 * both), columns(p_attend, 3 * both, 4 * both)
    w_pi, w_po = columns(p_conv, 0, 2 * both), columns(p_conv, 2 * both, 3 * both)
    w_late_up = columns(p_late, 0, hidden_cols)
    w_late_down = columns(p_late, hidden_cols, 2 * hidden_cols)

    stream0 = stream.astype(f32)
    stream1, saved_early = ffn_forward(stream0, gains[0], shifts[0], w_early_up, w_early_down)
    stream2, saved_attend = attention_forward(
        stream1, gains[1], shifts[1], w_att_in, w_att_out, table, meta
    )
    stream3, saved_conv = conv_forward(
        stream2, gains[2], shifts[2], w_pi, taps, w_po, cgain, cshift, meta
    )
    stream4, saved_late = ffn_forward(stream3, gains[4], shifts[4], w_late_up, w_late_down)
    result, unit5, r5 = norm_forward(stream4, gains[5], shifts[5])

    up = jnp.where(live[:, None], cotangent.astype(f32), 0.0)
    up, gain5, shift5 = norm_backward(up, unit5, r5, gains[5])
    up, g_late_up, g_late_down, gain4, shift4 = ffn_backward(
        up, gains[4], w_late_up, w_late_down, saved_late
    )
    g_late, signal = scatter_rows([g_late_up, g_late_down], None)
    up, g_conv, (g_taps, gain3, shift3), gain2, shift2 = conv_backward(
        up, gains[2], w_pi, taps, w_po, cgain, cshift, meta, saved_conv
    )
    g_conv, signal = scatter_rows(g_conv, signal)
    up, g_attend, g_table, gain1, shift1 = attention_backward(
        up, gains[1], w_att_in, w_att_out, table, meta, saved_attend
    )
    g_attend, signal = scatter_rows(g_attend, signal)
    up, g_early_up, g_early_down, gain0, shift0 = ffn_backward(
        up, gains[0], w_early_up, w_early_down, saved_early
    )
    g_early_down, signal = scatter_rows([g_early_down], signal)
    g_early_up, signal = scatter_rows([g_early_up], signal)

    def own_and_far(grad):
        own = [grad[:, at : at + channels] for at in range(0, grad.shape[1], both)]
        far = [grad[:, at + channels : at + both] for at in range(0, grad.shape[1], both)]
        far = to_far(jnp.concatenate(far, axis=1).astype(bf16)).astype(f32)
        return [o + far[:, n * channels : (n + 1) * channels] for n, o in enumerate(own)]

    g_q, g_k, g_v, g_out = own_and_far(g_attend)
    g_linear, g_gate, g_po = own_and_far(g_conv)

    result, norms = permute_blocks(
        [
            result.astype(bf16),
            jnp.stack([gain1, gain2, gain4, gain5, shift1, shift2, shift4, shift5]),
        ],
        inverse_order,
    )
    up, first = permute_blocks([up, jnp.stack([gain0, shift0] + [jnp.zeros((D,), f32)] * 6)], inverse_order)
    side = jnp.concatenate([g_taps, gain3[None], shift3[None]], axis=0)
    side = spread_channels(side[:, :channels], member) + spread_channels(side[:, channels:], far_member)
    g_table = g_table[:, :HEAD_DIM] + g_table[:, HEAD_DIM:]
    g_table = jnp.concatenate(
        [g_table[: RELS - 1], jnp.sum(g_table[RELS - 1 :], axis=0, keepdims=True)], axis=0
    )
    g_table = jnp.dot(selector.T, g_table, precision=highest)
    g_table = jnp.pad(g_table.reshape(-1), (0, 5 * D - RELS * HEAD_DIM)).reshape(5, D)
    sums = sum_everywhere(jnp.concatenate([norms, side, g_table], axis=0))
    first = sum_everywhere(first[:2])
    after_side = 8 + side.shape[0]
    side = sums[8:after_side]
    gains_all = jnp.concatenate([first[:1], sums[0:2], side[KERNEL : KERNEL + 1], sums[2:4]], axis=0)
    shifts_all = jnp.concatenate([first[1:], sums[4:6], side[KERNEL + 1 :], sums[6:8]], axis=0)
    table_all = sums[after_side:].reshape(-1)[: RELS * HEAD_DIM].reshape(RELS, HEAD_DIM)

    return (
        result,
        up,
        gains_all,
        shifts_all,
        g_early_up,
        g_early_down.T,
        jnp.stack([g_q, g_k, g_v]),
        g_out.T,
        table_all,
        jnp.stack([g_linear, g_gate], axis=1),
        side[:KERNEL],
        g_po.T,
        g_late[:, :hidden_cols],
        g_late[:, hidden_cols:].T,
    )


def solution(mesh):
    return jax.shard_map(
        per_device,
        mesh=mesh,
        in_specs=(
            P(("dp", "tensor"), None),
            P(),
            P(),
            P("dp", "tensor"),
            P("tensor", "dp"),
            P(None, "dp", "tensor"),
            P("tensor", "dp"),
            P(),
            P("dp", None, "tensor"),
            P(None, "tensor"),
            P("tensor", "dp"),
            P("dp", "tensor"),
            P("tensor", "dp"),
            P(("dp", "tensor"), None),
            P(),
            P(),
            P(),
        ),
        out_specs=(
            P(("dp", "tensor"), None),
            P(("dp", "tensor"), None),
            P(),
            P(),
            P("dp", "tensor"),
            P("tensor", "dp"),
            P(None, "dp", "tensor"),
            P("tensor", "dp"),
            P(),
            P("dp", None, "tensor"),
            P(),
            P("tensor", "dp"),
            P("dp", "tensor"),
            P("tensor", "dp"),
        ),
        check_vma=False,
    )
```

```python
import jax
import jax.numpy as jnp
from jax import lax
from jax.experimental import pallas as pl
from jax.experimental.pallas import tpu as pltpu
from jax.sharding import PartitionSpec as P

D = 1024
HEAD_DIM = 64
KERNEL = 31
REL_LEFT = 64
REL_RIGHT = 8
CLIP_DEV = 2
L = 512
HALF = L // 2
RELS = 73

norm_eps = 1e-05
masked_score = -1e30
highest = lax.Precision.HIGHEST
f32 = jnp.float32
bf16 = jnp.bfloat16

RING = (0, 2, 4, 6, 7, 5, 3, 1)


def mm(a, b):
    return jnp.dot(a, b, preferred_element_type=f32)


def mm_tn(a, b):
    return lax.dot_general(a, b, (((0,), (0,)), ((), ())), preferred_element_type=f32)


def mm_nt(a, b):
    return lax.dot_general(a, b, (((1,), (1,)), ((), ())), preferred_element_type=f32)


def swish(h):
    return h * jax.nn.sigmoid(h)


def swish_grad(h):
    s = jax.nn.sigmoid(h)
    return s * (1.0 + h * (1.0 - s))


def cost(micros):
    return pl.CostEstimate(
        flops=int(micros * 900_000_000), transcendentals=0, bytes_accessed=int(micros * 2_000_000)
    )


def to_core(v):
    return lax.ppermute(v, "tensor", [(m, m ^ 1) for m in range(lax.axis_size("tensor"))])


def to_far(v):
    return lax.ppermute(v, "tensor", [(m, m ^ 2) for m in range(lax.axis_size("tensor"))])


def to_right(v):
    n = len(RING)
    return lax.ppermute(v, "dp", [(RING[i], RING[(i + 1) % n]) for i in range(n)])


def to_left(v):
    n = len(RING)
    return lax.ppermute(v, "dp", [(RING[i], RING[(i - 1) % n]) for i in range(n)])


def on_ring():
    return lax.axis_size("dp") == len(RING)


def block_order():
    index = lax.axis_index("dp")
    count = lax.axis_size("dp")
    if not on_ring():
        return jnp.arange(count, dtype=jnp.int32)
    ring = jnp.array(RING, jnp.int32)
    place = jnp.sum(jnp.where(ring == index, jnp.arange(count, dtype=jnp.int32), 0))
    turned = (place + jnp.arange(count, dtype=jnp.int32)) % count
    return jnp.sum(jnp.where(turned[:, None] == jnp.arange(count)[None, :], ring[None, :], 0), axis=1)


def gather_rows(shard):
    if not on_ring():
        return [lax.all_gather(shard, "dp", axis=0, tiled=True)], [(shard,)] * 3
    half = shard.shape[0] // 2
    r1, l1 = to_right(shard), to_left(shard)
    r2, l2 = to_right(r1), to_left(l1)
    r3, l3 = to_right(r2), to_left(l2)
    r4, l4 = to_right(r3[:half]), to_left(l3[half:])
    return [shard, l1, l2, l3, r4, l4, r3, r2, r1], [(r1, l1), (r2, l2), (r3, l3)]


def scatter_rows(totals, order):
    count = lax.axis_size("dp")
    rows = totals[0].shape[0] // count
    if not on_ring():
        total = jnp.concatenate(totals, axis=1)
        return lax.psum_scatter(total, "dp", scatter_dimension=0, tiled=True).astype(f32)
    half = rows // 2

    def part(start, stop):
        at = order[start // rows] * rows + start % rows
        return jnp.concatenate(
            [lax.dynamic_slice_in_dim(t, at, stop - start) for t in totals], axis=1
        )

    def block(k):
        return part(k * rows, (k + 1) * rows)

    def plus(a, b):
        return (a.astype(f32) + b.astype(f32)).astype(bf16)

    right, left = part(4 * rows, 4 * rows + half), part(4 * rows + half, 5 * rows)
    m = to_right(right)
    n = to_left(left)
    m = to_right(
        jnp.concatenate(
            [plus(part(3 * rows, 3 * rows + half), m), part(3 * rows + half, 4 * rows)], axis=0
        )
    )
    n = to_left(
        jnp.concatenate(
            [part(5 * rows, 5 * rows + half), plus(part(5 * rows + half, 6 * rows), n)], axis=0
        )
    )
    m = to_right(plus(block(2), m))
    n = to_left(plus(block(6), n))
    m = to_right(plus(block(1), m))
    n = to_left(plus(block(7), n))
    return block(0).astype(f32) + m.astype(f32) + n.astype(f32)


def add_across(value, axis, bit):
    count = lax.axis_size(axis)
    return value + lax.ppermute(value, axis, [(m, m ^ bit) for m in range(count)])


def sum_groups(value):
    steps = [add_across(value, "tensor", 2)]
    bit = 1
    while bit < lax.axis_size("dp"):
        steps.append(add_across(steps[-1], "dp", bit))
        bit *= 2
    return steps


def gather_queued(shard):
    return lax.all_gather(shard, "dp", axis=0, tiled=True)


def scatter_queued(total):
    return lax.psum_scatter(total, "dp", scatter_dimension=0, tiled=True).astype(f32)


def gather_clip(mine):
    return jnp.concatenate([mine, to_core(mine)], axis=0)


def reduce_clip(partial):
    rows = partial.shape[0] // 2
    partial = partial.astype(bf16)
    return partial[:rows].astype(f32) + to_core(partial[rows:]).astype(f32)


def gather_frames(mine):
    near = to_core(mine)
    far = to_far(mine)
    return jnp.concatenate([mine, near], axis=0), jnp.concatenate([far, to_core(far)], axis=0)


def send_other(other):
    rows = other.shape[0] // 2
    other = other.astype(bf16)
    near = to_core(other[rows:])
    summed = (other[:rows].astype(f32) + near.astype(f32)).astype(bf16)
    return to_far(summed), summed


def reduce_own(own, far):
    rows = own.shape[0] // 2
    own = own.astype(bf16)
    return own[:rows].astype(f32) + to_core(own[rows:]).astype(f32) + far.astype(f32)


ANY = pl.BlockSpec(memory_space=pl.ANY)


def after(values, tokens):
    def body(*refs):
        pass

    tokens = list(tokens)
    return pl.pallas_call(
        body,
        in_specs=[ANY] * (len(values) + len(tokens)),
        out_specs=[ANY] * len(values),
        out_shape=[jax.ShapeDtypeStruct(v.shape, v.dtype) for v in values],
        input_output_aliases={n: n for n in range(len(values))},
    )(*values, *tokens)


def assemble(pieces, order, spans):
    if not on_ring():
        return [pieces[0][:, start:stop] for start, stop in spans]
    block = pieces[0].shape[0]
    half = block // 2
    shapes = [
        jax.ShapeDtypeStruct((block * order.shape[0], stop - start), pieces[0].dtype)
        for start, stop in spans
    ]
    places = ((0, 0), (1, 0), (2, 0), (3, 0), (4, 0), (4, half), (5, 0), (6, 0), (7, 0))

    def body(order_ref, *refs):
        ins, outs = refs[: len(pieces)], refs[len(pieces) :]
        for src, (place, first) in zip(ins, places):
            to = pl.multiple_of(order_ref[place] * block + first, half)
            for dst, (start, stop) in zip(outs, spans):
                dst[pl.ds(to, src.shape[0]), :] = src[:, start:stop]

    return pl.pallas_call(
        body,
        grid_spec=pltpu.PrefetchScalarGridSpec(
            num_scalar_prefetch=1,
            grid=(),
            in_specs=[pl.BlockSpec(memory_space=pltpu.VMEM) for _ in pieces],
            out_specs=[pl.BlockSpec(memory_space=pltpu.VMEM) for _ in spans],
        ),
        out_shape=shapes,
        cost_estimate=cost(4),
    )(order, *pieces)


def norm_forward(v, gain, shift):
    centre = v - jnp.mean(v, axis=-1, keepdims=True)
    spread = jnp.mean(centre * centre, axis=-1, keepdims=True)
    r = lax.rsqrt(spread + norm_eps)
    unit = centre * r
    return unit * gain + shift, unit, r


def norm_backward(q, unit, r, gain):
    scaled = q * gain
    bracket = (
        scaled
        - jnp.mean(scaled, axis=-1, keepdims=True)
        - unit * jnp.mean(scaled * unit, axis=-1, keepdims=True)
    )
    return r * bracket, jnp.sum(q * unit, axis=0), jnp.sum(q, axis=0)


def ffn_forward(stream, gain, shift, up, down_t):
    normed, unit, r = norm_forward(stream, gain, shift)
    frames, other = gather_frames(normed.astype(bf16))

    def half(x):
        hidden = mm(x, up)
        active = swish(hidden).astype(bf16)
        return hidden, active, mm_nt(active, down_t)

    hidden_other, active_other, part = half(other)
    far, sent = send_other(part)
    (frames,) = after([frames], [sent])
    hidden, active, part = half(frames)
    branch = reduce_own(part, far)
    saved = (unit, r, (frames, other), (hidden, hidden_other), (active, active_other))
    return stream + 0.5 * branch, saved


def ffn_backward(upstream, gain, up, down_t, saved, wait):
    unit, r, frames, hidden, active = saved
    incoming, other = gather_frames(upstream.astype(bf16))

    def half(g, h):
        d = (0.5 * mm(g, down_t) * swish_grad(h)).astype(bf16)
        return d, mm_nt(d, up)

    d_other, part = half(other, hidden[1])
    far, sent = send_other(part)
    (incoming,) = after([incoming], [sent])
    d_own, part = half(incoming, hidden[0])
    dnormed = reduce_own(part, far)
    if wait:
        *frames, active_own, active_other = after([*frames, *active], [sent])
        active = active_own, active_other
    grad_down = (0.5 * (mm_tn(incoming, active[0]) + mm_tn(other, active[1]))).astype(bf16)
    grad_up = (mm_tn(frames[0], d_own) + mm_tn(frames[1], d_other)).astype(bf16)
    dstream, dgain, dshift = norm_backward(dnormed, unit, r, gain)
    return upstream + dstream, grad_up, grad_down, dgain, dshift


LANES = 128
SCALE = HEAD_DIM ** (-0.5)


def head_lanes(value, upper):
    lane = lax.broadcasted_iota(jnp.int32, value.shape, 1)
    return jnp.where((lane >= HEAD_DIM) == upper, value, jnp.zeros_like(value))


def either(first, second):
    lane = lax.broadcasted_iota(jnp.int32, first.shape, 1)
    return jnp.where(lane < HEAD_DIM, first, second)


def tile_probs(meta_ref, q, k, table):
    low, length = meta_ref[0], meta_ref[1]
    place_i = (lax.broadcasted_iota(jnp.int32, (L, L), 0) + low * HALF) & (L - 1)
    place_j = (lax.broadcasted_iota(jnp.int32, (L, L), 1) + low * HALF) & (L - 1)
    offset = place_j - place_i
    by_row = mm_nt(q, table)
    turned = pltpu.roll(by_row, REL_LEFT, 1, stride=1, stride_axis=0)
    turned = jnp.concatenate([turned] * (L // LANES), axis=1)
    relative = jnp.where(
        offset < -REL_LEFT,
        by_row[:, :1],
        jnp.where(offset >= LANES - REL_LEFT, by_row[:, LANES - 1 :], turned),
    )
    scores = mm_nt(q, k) + relative
    scores = jnp.where(place_j < length, scores, masked_score)
    raised = jnp.exp(scores - jnp.max(scores, axis=-1, keepdims=True))
    return raised * (1.0 / jnp.sum(raised, axis=-1, keepdims=True)), offset


def attend_body(meta_ref, q_ref, k_ref, v_ref, table_ref, *rest):
    out_ref = rest[-1]
    q, k, v, table = q_ref[...] * SCALE, k_ref[...], v_ref[...], table_ref[...]
    outs = []
    for upper in (False, True):
        shares, _ = tile_probs(meta_ref, head_lanes(q, upper), k, table)
        outs.append(mm(shares.astype(bf16), v))
    out_ref[...] = either(*outs).astype(bf16)


def pair_specs(pairs, first=0):
    def at(which):
        return pl.BlockSpec((L, LANES), lambda n, meta: (0, which * pairs + first + n))

    return [at(0), at(1), at(2)]


def attend(qkv, table, meta, part, tokens):
    width = qkv.shape[1] // 6
    pairs = width // LANES
    return pl.pallas_call(
        attend_body,
        grid_spec=pltpu.PrefetchScalarGridSpec(
            num_scalar_prefetch=1,
            grid=(pairs,),
            in_specs=pair_specs(2 * pairs, part * pairs)
            + [pl.BlockSpec((LANES, LANES), lambda n, meta: (0, 0))]
            + [ANY] * len(tokens),
            out_specs=pl.BlockSpec((L, LANES), lambda n, meta: (0, n)),
        ),
        out_shape=jax.ShapeDtypeStruct((L, width), bf16),
        cost_estimate=cost(8),
    )(meta, qkv, qkv, qkv, table, *tokens)


def attend_back_body(
    meta_ref, q_ref, k_ref, v_ref, do_ref, table_ref, dq_ref, dk_ref, dv_ref, dtable_ref
):
    q, k, v, do, table = q_ref[...] * SCALE, k_ref[...], v_ref[...], do_ref[...], table_ref[...]
    lane = lax.broadcasted_iota(jnp.int32, (L, LANES), 1)
    row = lax.broadcasted_iota(jnp.int32, (L, LANES), 0)
    dqs, dks, dvs = [], [], []
    dtable = jnp.zeros((LANES, LANES), f32)
    for upper in (False, True):
        q_one = head_lanes(q, upper)
        shares, offset = tile_probs(meta_ref, q_one, k, table)
        dvs.append(mm_tn(shares.astype(bf16), do))
        dshares = mm_nt(head_lanes(do, upper), v)
        centre = jnp.sum(shares * dshares, axis=-1, keepdims=True)
        ds = (shares * (dshares - centre)).astype(bf16)
        wide = ds.astype(f32)
        before = offset < -REL_LEFT
        beyond = offset >= LANES - REL_LEFT
        left = jnp.sum(jnp.where(before, wide, 0.0), axis=-1, keepdims=True)
        right = jnp.sum(jnp.where(beyond, wide, 0.0), axis=-1, keepdims=True)
        band = jnp.where(before | beyond, 0.0, wide)
        pulled = sum(band[:, n * LANES : (n + 1) * LANES] for n in range(L // LANES))
        pulled = pltpu.roll(pulled, LANES - REL_LEFT, 1)
        bit = 1
        while bit < LANES:
            pulled = jnp.where((row & bit) != 0, pltpu.roll(pulled, LANES - bit, 1), pulled)
            bit *= 2
        pulled = pulled + jnp.where(lane == 0, left, 0.0) + jnp.where(lane == LANES - 1, right, 0.0)
        pulled = pulled.astype(bf16)
        dqs.append(mm(ds, k) + mm(pulled, table))
        dks.append(mm_tn(ds, q))
        dtable = dtable + mm_tn(pulled, q_one)
    dq_ref[...] = (either(*dqs) * SCALE).astype(bf16)
    dk_ref[...] = either(*dks).astype(bf16)
    dv_ref[...] = either(*dvs).astype(bf16)

    @pl.when(pl.program_id(0) == 0)
    def _():
        dtable_ref[...] = jnp.zeros_like(dtable_ref)

    dtable_ref[...] += dtable


def attend_back(qkv, dout, table, meta, part, tokens):
    width = qkv.shape[1] // 6
    pairs = width // LANES
    pair = pl.BlockSpec((L, LANES), lambda n, meta: (0, n))
    pair_in = pl.BlockSpec((L, LANES), lambda n, meta: (0, part * pairs + n))
    square = pl.BlockSpec((LANES, LANES), lambda n, meta: (0, 0))
    one = jax.ShapeDtypeStruct((L, width), bf16)
    return pl.pallas_call(
        lambda *refs: attend_back_body(*refs[:6], *refs[6 + len(tokens) :]),
        grid_spec=pltpu.PrefetchScalarGridSpec(
            num_scalar_prefetch=1,
            grid=(pairs,),
            in_specs=pair_specs(2 * pairs, part * pairs) + [pair_in, square] + [ANY] * len(tokens),
            out_specs=[pair, pair, pair, square],
        ),
        out_shape=[one, one, one, jax.ShapeDtypeStruct((LANES, LANES), f32)],
        cost_estimate=cost(14),
    )(meta, qkv, qkv, qkv, dout, table, *tokens)


def attention_forward(stream, gain, shift, w_in, w_out_t, table, meta, signals):
    normed, unit, r = norm_forward(stream, gain, shift)
    frames = gather_clip(normed.astype(bf16))
    qkv = mm(frames, w_in).astype(bf16)
    attended = [attend(qkv, table, meta, n, signals[n]) for n in (0, 1)]
    attended = jnp.concatenate(attended, axis=1)
    branch = reduce_clip(mm_nt(attended, w_out_t))
    return stream + branch, (unit, r, frames, qkv, attended)


def attention_backward(upstream, gain, w_in, w_out_t, table, meta, saved, signals):
    unit, r, frames, qkv, attended = saved
    incoming = gather_clip(upstream.astype(bf16))
    datt = mm(incoming, w_out_t).astype(bf16)
    halves = [attend_back(qkv, datt, table, meta, n, signals[n]) for n in (0, 1)]
    dqkv = jnp.concatenate([halves[n][which] for which in (0, 1, 2) for n in (0, 1)], axis=1)
    dtable = halves[0][3] + halves[1][3]
    dnormed = reduce_clip(mm_nt(dqkv, w_in))
    dstream, dgain, dshift = norm_backward(dnormed, unit, r, gain)
    upstream = upstream + dstream
    sent = upstream.astype(bf16)
    frames, attended = after([frames, attended], [sent])
    grads = [mm_tn(frames, dqkv).astype(bf16), mm_tn(incoming, attended).astype(bf16)]
    return upstream, grads, dtable, dgain, dshift


PAD = 32
CHUNK = 64


def place_rows(dst, value, start, low):
    own = pl.multiple_of(start + low * HALF, 8)
    other = pl.multiple_of(start + (1 - low) * HALF, 8)
    dst[pl.ds(own, HALF), :] = value[:HALF]
    dst[pl.ds(other, HALF), :] = value[HALF:]


def taken_rows(src, start, low):
    own = pl.multiple_of(start + low * HALF, 8)
    other = pl.multiple_of(start + (1 - low) * HALF, 8)
    return src[pl.ds(own, HALF), :], src[pl.ds(other, HALF), :]


def shifted(window, shift):
    size = window.shape[0]
    turned = {}

    def at(first):
        part = first % 8
        if part not in turned:
            turned[part] = window if part == 0 else pltpu.roll(window, size - part, 0)
        base = first - part
        return turned[part][base : base + CHUNK]

    return at


def conv_body(meta_ref, linear_ref, gate_ref, taps_ref, *rest):
    out_ref, padded, placed = rest[-3:]
    low = meta_ref[0]
    padded[:PAD, :] = jnp.zeros((PAD, LANES), f32)
    place_rows(padded, linear_ref[...] * jax.nn.sigmoid(gate_ref[...]), PAD, low)
    taps = taps_ref[...]

    def chunk(c, carry):
        base = pl.multiple_of(c * CHUNK, CHUNK)
        at = shifted(padded[pl.ds(base, CHUNK + PAD), :], 0)
        total = taps[0:1] * at(2)
        for k in range(1, KERNEL):
            total = total + taps[k : k + 1] * at(2 + k)
        placed[pl.ds(base, CHUNK), :] = total
        return carry

    lax.fori_loop(0, L // CHUNK, chunk, 0)
    out_ref[:HALF, :], out_ref[HALF:, :] = taken_rows(placed, 0, low)


def conv_back_body(
    meta_ref, dconv_ref, linear_ref, gate_ref, taps_ref, dlin_ref, dgate_ref, dtaps_ref, padded, late, placed
):
    low = meta_ref[0]
    linear, opened = linear_ref[...], jax.nn.sigmoid(gate_ref[...])
    padded[:PAD, :] = jnp.zeros((PAD, LANES), f32)
    place_rows(padded, linear * opened, PAD, low)
    late[L:, :] = jnp.zeros((PAD, LANES), f32)
    place_rows(late, dconv_ref[...], 0, low)
    taps = taps_ref[...]
    dtaps_ref[...] = jnp.zeros_like(dtaps_ref)

    def chunk(c, carry):
        base = pl.multiple_of(c * CHUNK, CHUNK)
        window = late[pl.ds(base, CHUNK + PAD), :]
        ahead = shifted(window, 0)
        back = shifted(padded[pl.ds(base, CHUNK + PAD), :], 0)
        here = window[:CHUNK]
        total = taps[KERNEL - 1 : KERNEL] * here
        for k in range(KERNEL - 1):
            total = total + taps[k : k + 1] * ahead(KERNEL - 1 - k)
        placed[pl.ds(base, CHUNK), :] = total
        for k in range(KERNEL):
            part = (back(2 + k) * here).reshape(CHUNK // 8, 8, LANES)
            dtaps_ref[8 * k : 8 * k + 8, :] += jnp.sum(part, axis=0)
        return carry

    lax.fori_loop(0, L // CHUNK, chunk, 0)
    dgated = jnp.concatenate(taken_rows(placed, 0, low), axis=0)
    dlin_ref[...] = (dgated * opened).astype(bf16)
    dgate_ref[...] = (dgated * linear * opened * (1.0 - opened)).astype(bf16)


def conv_specs(blocks):
    linear = pl.BlockSpec((L, LANES), lambda n, meta: (0, n))
    gate = pl.BlockSpec((L, LANES), lambda n, meta: (0, blocks + n))
    taps = pl.BlockSpec((PAD, LANES), lambda n, meta: (0, n))
    return linear, gate, taps


def conv_gated(halves, taps, meta, tokens):
    width = halves.shape[1] // 2
    linear, gate, tap = conv_specs(width // LANES)
    return pl.pallas_call(
        conv_body,
        grid_spec=pltpu.PrefetchScalarGridSpec(
            num_scalar_prefetch=1,
            grid=(width // LANES,),
            in_specs=[linear, gate, tap] + [ANY] * len(tokens),
            out_specs=linear,
            scratch_shapes=[pltpu.VMEM((L + PAD, LANES), f32), pltpu.VMEM((L, LANES), f32)],
        ),
        out_shape=jax.ShapeDtypeStruct((L, width), f32),
        cost_estimate=cost(6),
    )(meta, halves, halves, taps, *tokens)


def conv_gated_back(dconv, halves, taps, meta):
    width = dconv.shape[1]
    linear, gate, tap = conv_specs(width // LANES)
    long = pltpu.VMEM((L + PAD, LANES), f32)
    return pl.pallas_call(
        conv_back_body,
        grid_spec=pltpu.PrefetchScalarGridSpec(
            num_scalar_prefetch=1,
            grid=(width // LANES,),
            in_specs=[linear, linear, gate, tap],
            out_specs=[linear, linear, pl.BlockSpec((8 * PAD, LANES), lambda n, meta: (0, n))],
            scratch_shapes=[long, long, pltpu.VMEM((L, LANES), f32)],
        ),
        out_shape=[
            jax.ShapeDtypeStruct((L, width), bf16),
            jax.ShapeDtypeStruct((L, width), bf16),
            jax.ShapeDtypeStruct((8 * PAD, width), f32),
        ],
        cost_estimate=cost(10),
    )(meta, dconv, halves, halves, taps)


def near_rows(pair):
    return jnp.roll(to_core(pair), HALF, axis=-1)


def channel_stats(convolved):
    count = convolved.shape[1]
    mean = jnp.mean(convolved, axis=-1)
    centre = convolved - mean[:, None]
    pair = jnp.stack([mean, jnp.sum(centre * centre, axis=-1)])
    other = near_rows(pair)
    gap = pair[0] - other[0]
    mean = 0.5 * (pair[0] + other[0])
    spread = (pair[1] + other[1] + 0.5 * count * gap * gap) / (2 * count)
    return mean[:, None], lax.rsqrt(spread + norm_eps)[:, None]


def conv_forward(stream, gain, shift, w_in, taps, w_out_t, cgain, cshift, meta, signal):
    normed, unit, r = norm_forward(stream, gain, shift)
    frames = gather_clip(normed.astype(bf16))
    halves = mm(frames, w_in)
    convolved = conv_gated(halves, taps, meta, signal)
    mean, inverse = channel_stats(convolved)
    cunit = (convolved - mean) * inverse
    active = swish(cunit * cgain + cshift).astype(bf16)
    branch = reduce_clip(mm_nt(active, w_out_t))
    return stream + branch, (unit, r, frames, halves, cunit, inverse, active)


def conv_backward(upstream, gain, w_in, taps, w_out_t, cgain, cshift, meta, saved):
    unit, r, frames, halves, cunit, inverse, active = saved
    incoming = gather_clip(upstream.astype(bf16))
    dmid = mm(incoming, w_out_t) * swish_grad(cunit * cgain + cshift)
    scaled = dmid * cgain
    pair = jnp.stack([jnp.sum(scaled, axis=-1), jnp.sum(scaled * cunit, axis=-1)])
    pair = (pair + near_rows(pair)) / D
    dconv = inverse * (scaled - pair[0][:, None] - cunit * pair[1][:, None])
    dlin, dgate, dtaps = conv_gated_back(dconv, halves, taps, meta)
    width = dlin.shape[1]
    dnormed = reduce_clip(mm_nt(dlin, w_in[:, :width]) + mm_nt(dgate, w_in[:, width:]))
    grads = [mm_tn(frames, d).astype(bf16) for d in (dlin, dgate)]
    grads.append(mm_tn(incoming, active).astype(bf16))
    dtaps = jnp.sum(dtaps.reshape(PAD, 8, width), axis=1)[:KERNEL]
    sums = (dtaps, jnp.sum(dmid * cunit, axis=0), jnp.sum(dmid, axis=0))
    dstream, dgain, dshift = norm_backward(dnormed, unit, r, gain)
    return upstream + dstream, grads, sums, dgain, dshift


def per_device(
    layer_in,
    norm_gain,
    norm_shift,
    early_up,
    early_down,
    attend_in,
    attend_out,
    position_table,
    pointwise_in,
    depthwise,
    pointwise_out,
    late_up,
    late_down,
    output_grad,
    clip_lengths,
    clip_slots,
    position_rows,
):
    group = lax.axis_index("dp")
    member = lax.axis_index("tensor")
    low = member % 2
    high = member // 2
    rows_here = layer_in.shape[0]
    block = early_up.shape[0]
    channels = depthwise.shape[1]

    order = block_order()
    gains, shifts = norm_gain, norm_shift

    slot = group * CLIP_DEV + high
    length = jnp.sum(jnp.where(clip_slots == slot, clip_lengths, 0))
    live = low * rows_here + jnp.arange(rows_here, dtype=jnp.int32) < length
    meta = jnp.stack([low, length]).astype(jnp.int32)

    selector = (position_rows[:, None] == jnp.arange(RELS, dtype=jnp.int32)[None, :]).astype(f32)
    table = jnp.dot(selector, position_table.astype(f32), precision=highest).astype(bf16)
    table = jnp.concatenate([table, jnp.broadcast_to(table[-1:], (LANES - RELS, HEAD_DIM))], axis=0)
    table = jnp.concatenate([table, table], axis=1)

    far_member = member ^ 2

    def both_members(row):
        return jnp.concatenate(
            [
                lax.dynamic_slice_in_dim(row, at * channels, channels)
                for at in (member, far_member)
            ]
        )

    cgain, cshift = both_members(norm_gain[3]), both_members(norm_shift[3])

    pack_attend = jnp.concatenate(
        [jnp.moveaxis(attend_in, 0, 1).reshape(block, -1), attend_out.T], axis=1
    )
    pack_conv = jnp.concatenate([pointwise_in.reshape(block, -1), pointwise_out.T], axis=1)
    far_attend = to_far(pack_attend)
    taps = jnp.concatenate([depthwise, to_far(depthwise)], axis=1).astype(f32)
    taps = jnp.pad(taps, ((0, PAD - KERNEL), (0, 0)))

    def paired(own, far):
        parts = []
        for at in range(0, own.shape[1], channels):
            parts += [own[:, at : at + channels], far[:, at : at + channels]]
        return jnp.concatenate(parts, axis=1)

    both = 2 * channels
    hidden_cols = early_up.shape[1]
    p_early, signals = gather_rows(jnp.concatenate([early_up, early_down.T], axis=1))
    p_attend, signals_attend = gather_rows(paired(pack_attend, far_attend))
    shard_conv, shard_up = after([pack_conv, late_up], signals[2])
    w_conv = gather_queued(shard_conv)
    w_late_up = gather_queued(shard_up)
    p_late_down, signals = gather_rows(after([late_down.T], signals_attend[2])[0])
    (w_late_down,) = assemble(p_late_down, order, [(0, hidden_cols)])
    w_early_up, w_early_down = assemble(
        p_early, order, [(0, hidden_cols), (hidden_cols, 2 * hidden_cols)]
    )
    w_att_in, w_att_out = assemble(p_attend, order, [(0, 3 * both), (3 * both, 4 * both)])
    far_conv = to_far(w_conv)
    w_conv = paired(w_conv, far_conv)
    w_pi, w_po = w_conv[:, : 2 * both], w_conv[:, 2 * both :]

    stream0 = layer_in.astype(f32)
    stream1, saved_early = ffn_forward(stream0, gains[0], shifts[0], w_early_up, w_early_down)
    stream2, saved_attend = attention_forward(
        stream1, gains[1], shifts[1], w_att_in, w_att_out, table, meta, [signals[0], [*signals[1], far_conv]]
    )
    stream3, saved_conv = conv_forward(
        stream2, gains[2], shifts[2], w_pi, taps, w_po, cgain, cshift, meta, [*signals[2], w_late_up]
    )
    stream4, saved_late = ffn_forward(stream3, gains[4], shifts[4], w_late_up, w_late_down)
    result, unit5, r5 = norm_forward(stream4, gains[5], shifts[5])

    up = jnp.where(live[:, None], output_grad.astype(f32), 0.0)
    up, gain5, shift5 = norm_backward(up, unit5, r5, gains[5])
    up, g_late_up, g_late_down, gain4, shift4 = ffn_backward(
        up, gains[4], w_late_up, w_late_down, saved_late, True
    )
    g_late_up = scatter_queued(g_late_up)
    g_late_down = scatter_queued(g_late_down)
    up, g_conv, (g_taps, gain3, shift3), gain2, shift2 = conv_backward(
        up, gains[2], w_pi, taps, w_po, cgain, cshift, meta, saved_conv
    )
    norms = jnp.stack([gain2, gain4, gain5, shift2, shift4, shift5]).reshape(-1, both)
    side = jnp.concatenate([g_taps, gain3[None], shift3[None]], axis=0)
    side = jnp.where(high == 0, side, jnp.roll(side, channels, axis=1))
    steps = sum_groups(jnp.concatenate([norms, side], axis=0))
    own, far = [
        jnp.concatenate([g[:, at : at + channels] for g in g_conv], axis=1) for at in (0, channels)
    ]
    g_conv = scatter_queued((own.astype(f32) + to_far(far).astype(f32)).astype(bf16))
    up, g_attend, g_table, gain1, shift1 = attention_backward(
        up, gains[1], w_att_in, w_att_out, table, meta, saved_attend, [(), [steps[1]]]
    )
    g_attend = scatter_rows(g_attend, order)
    up, g_early_up, g_early_down, gain0, shift0 = ffn_backward(
        up, gains[0], w_early_up, w_early_down, saved_early, False
    )
    g_early_down = scatter_rows([g_early_down], order)
    g_early_up = scatter_rows([g_early_up], order)

    def own_and_far(grad):
        own = [grad[:, at : at + channels] for at in range(0, grad.shape[1], both)]
        far = [grad[:, at + channels : at + both] for at in range(0, grad.shape[1], both)]
        far = to_far(jnp.concatenate(far, axis=1).astype(bf16)).astype(f32)
        return [o + far[:, n * channels : (n + 1) * channels] for n, o in enumerate(own)]

    g_q, g_k, g_v, g_out = own_and_far(g_attend)
    g_linear, g_gate, g_po = [g_conv[:, at : at + channels] for at in (0, channels, both)]

    result = result.astype(bf16)
    g_table = g_table[:, :HEAD_DIM] + g_table[:, HEAD_DIM:]
    g_table = jnp.concatenate(
        [g_table[: RELS - 1], jnp.sum(g_table[RELS - 1 :], axis=0, keepdims=True)], axis=0
    )
    g_table = jnp.dot(selector.T, g_table, precision=highest)
    g_table = jnp.pad(g_table.reshape(-1), (0, 5 * D - RELS * HEAD_DIM)).reshape(5, D)
    last = sum_groups(jnp.concatenate([jnp.stack([gain0, gain1, shift0, shift1]), g_table], axis=0))
    last = add_across(last[-1], "tensor", 1)
    sums, near = steps[-1], to_core(steps[-1])
    count = norms.shape[0]
    norms = (sums[:count] + near[:count]).reshape(-1, D)
    first = jnp.where(low == 0, sums[count:], near[count:])
    second = jnp.where(low == 0, near[count:], sums[count:])
    side = jnp.concatenate(
        [part[:, at : at + channels] for at in (0, channels) for part in (first, second)], axis=1
    )
    gains_all = jnp.concatenate(
        [last[0:2], norms[0:1], side[KERNEL : KERNEL + 1], norms[1:3]], axis=0
    )
    shifts_all = jnp.concatenate([last[2:4], norms[3:4], side[KERNEL + 1 :], norms[4:6]], axis=0)
    table_all = last[4:].reshape(-1)[: RELS * HEAD_DIM].reshape(RELS, HEAD_DIM)

    return (
        result,
        up,
        gains_all,
        shifts_all,
        g_early_up,
        g_early_down.T,
        jnp.stack([g_q, g_k, g_v]),
        g_out.T,
        table_all,
        jnp.stack([g_linear, g_gate], axis=1),
        side[:KERNEL],
        g_po.T,
        g_late_up,
        g_late_down.T,
    )


def solution(mesh):
    return jax.shard_map(
        per_device,
        mesh=mesh,
        in_specs=(
            P(("dp", "tensor"), None),
            P(),
            P(),
            P("dp", "tensor"),
            P("tensor", "dp"),
            P(None, "dp", "tensor"),
            P("tensor", "dp"),
            P(),
            P("dp", None, "tensor"),
            P(None, "tensor"),
            P("tensor", "dp"),
            P("dp", "tensor"),
            P("tensor", "dp"),
            P(("dp", "tensor"), None),
            P(),
            P(),
            P(),
        ),
        out_specs=(
            P(("dp", "tensor"), None),
            P(("dp", "tensor"), None),
            P(),
            P(),
            P("dp", "tensor"),
            P("tensor", "dp"),
            P(None, "dp", "tensor"),
            P("tensor", "dp"),
            P(),
            P("dp", None, "tensor"),
            P(),
            P("tensor", "dp"),
            P("dp", "tensor"),
            P("tensor", "dp"),
        ),
        check_vma=False,
    )
```
